32 devices in a mesh: wide: 16 (over z, y, x), narrow: 2 (over core).
Axes of the slice: x: 2, y: 2, z: 4, core: 2. Of those that a mesh axis runs over, the one named last changes fastest.
Arguments:
- blocks: float32 [256, 14, 128, 128], P('wide', 'narrow'), may hold values from -0.125 to 0.125
- vectors: float32 [32768, 512], P('wide'), may hold values from -1.5 to 1.5
- sign_bits: int32 [32768], P('wide'), may hold values from 0 to 1
- column_blocks: int32 [256, 14], P('wide', 'narrow'), may hold values from 0 to 255, as said below
- sample_rows: int32 [1024], P('wide'), may hold values from 0 to 32767, as said below
Outputs:
- sketch: float32 [1024, 512], P('wide', 'narrow')
The draws below stay inside these ranges and needn't reach their ends.
Inputs may be any that keep to these rules, and one draw needn't show every extreme that they name: `column_blocks`: entry [g, j] equals (g + o) mod 256 for an offset o with -8 <= o <= 8; both offsets -8 and 8 occur in every draw. `sample_rows`: entries 64 * w to 64 * w + 63 are distinct rows of slab w, that is of rows 16 * 128 * w to 16 * 128 * w + 16 * 128 - 1, in increasing order.
All inputs are finite; a program needn't handle non-finite values.
Results may differ from the reference program's by a relative error of at most 0.00013.
Values sent between devices are 32-bit elements; how exact they have to be, the bound alone decides.
A program may use at most 192 MiB of HBM per device.

```python
import math
import jax
import jax.numpy as jnp
from jax import lax

BLK = 128
NNZB = 14
KCOL = 512
REACH = 8
BR_DEV = 16
S_DEV = 64
NB = 256
NN = 32768
SAMPLES = 1024
N_WIDE = 16


def draw_column_blocks(key, part):
    total_blocks = BR_DEV * N_WIDE
    offsets = jax.random.randint(key, (total_blocks, NNZB), -REACH, REACH + 1, dtype=jnp.int32)
    offsets = offsets.at[0, 0].set(-REACH)
    offsets = offsets.at[total_blocks - 1, 1].set(REACH)
    offsets = offsets.at[0, 2].set(-1)
    offsets = offsets.at[total_blocks - 1, 3].set(1)
    block_rows = jnp.arange(total_blocks, dtype=jnp.int32)[:, None]
    return ((block_rows + offsets) % total_blocks).astype(jnp.int32)


def draw_sample_rows(key, part):
    rows_slab = BR_DEV * BLK
    slab_keys = jax.random.split(key, N_WIDE)

    def one_slab(slab_key):
        return jnp.sort(jax.random.permutation(slab_key, rows_slab)[:S_DEV])
    local_rows = jax.vmap(one_slab)(slab_keys).astype(jnp.int32)
    local_rows = local_rows.at[0, 0].set(0)
    local_rows = local_rows.at[N_WIDE - 1, S_DEV - 1].set(rows_slab - 1)
    slab_starts = (jnp.arange(N_WIDE, dtype=jnp.int32) * rows_slab)[:, None]
    return (local_rows + slab_starts).reshape(-1).astype(jnp.int32)


def place_ends(values, stream_key, least, high):
    spot = [jax.random.randint(jax.random.fold_in(stream_key, axis), (), 0, length) for axis, length in enumerate(values.shape)]
    longest = values.shape.index(max(values.shape))
    next_to = spot[:longest] + [(spot[longest] + 1) % values.shape[longest]] + spot[longest + 1:]
    return values.at[tuple(spot)].set(least).at[tuple(next_to)].set(high)


def level_of(rng, dims, cuts, smallest, largest):
    def one(dim, shards_of):
        steps = jax.random.uniform(jax.random.fold_in(jax.random.fold_in(rng, 6), dim), (shards_of,), jnp.float32, smallest / len(cuts), largest / len(cuts))
        return jnp.repeat(jnp.exp(steps), dims[dim] // shards_of).reshape((-1,) + (1,) * (len(dims) - dim - 1))

    loudness = one(*cuts[0])
    for cut in cuts[1:]:
        loudness = loudness * one(*cut)
    return loudness


def normal_values(stream_key, extent, width, most, cuts=(), kind=jnp.bfloat16):
    level = level_of(stream_key, extent, cuts, -0.22, 0.18) if cuts else 1.0
    values = jax.random.normal(stream_key, extent, jnp.float32) * width * level
    return jnp.minimum(jnp.maximum(values, -most), most).astype(kind)


def setup_inputs(seed: int = 0) -> dict:
    streams_of = jax.random.split(jax.random.key(seed), 6)
    return {
        "blocks": normal_values(streams_of[0], (NB, NNZB, BLK, BLK), (NNZB * BLK) ** -0.5, 0.125, ((0, 16), (1, 2)), jnp.float32),
        "vectors": normal_values(streams_of[1], (NN, KCOL), 0.25, 1.5, ((0, 16),), jnp.float32),
        "sign_bits": place_ends(jax.random.randint(streams_of[2], (NN,), 0, 2), jax.random.fold_in(streams_of[2], 1), 0, 1).astype(jnp.int32),
        "column_blocks": draw_column_blocks(jax.random.fold_in(streams_of[5], 71), 0),
        "sample_rows": draw_sample_rows(jax.random.fold_in(streams_of[5], 71), 0),
    }


def sylvester_matrix(order):
    positions = jnp.arange(order, dtype=jnp.int32)
    common = positions[:, None] & positions[None, :]
    parity = jnp.zeros((order, order), jnp.int32)
    for shift_bits in range(max(order - 1, 1).bit_length()):
        parity = parity + (common >> shift_bits & 1)
    return (1 - 2 * (parity % 2)).astype(jnp.float32)

def reference(blocks, vectors, sign_bits, column_blocks, sample_rows):
    highest = lax.Precision.HIGHEST
    vector_blocks = vectors.reshape(NB, BLK, KCOL)
    slab_blocks = blocks.reshape(N_WIDE, BR_DEV, NNZB, BLK, BLK)
    slab_columns = column_blocks.reshape(N_WIDE, BR_DEV, NNZB)

    def slab_product(pieces):
        block_slab, column_slab = pieces
        picked = vector_blocks[column_slab]
        return jnp.einsum('bjik,bjkn->bin', block_slab, picked, precision=highest)
    product = lax.map(slab_product, (slab_blocks, slab_columns))
    signs = (2 * sign_bits - 1).astype(jnp.float32).reshape(N_WIDE, BR_DEV, BLK, 1)
    signed = product * signs
    local_mix = jnp.einsum('ik,wbkn->wbin', sylvester_matrix(BLK), signed, precision=highest)
    mixed = jnp.einsum('wv,vbin->wbin', sylvester_matrix(N_WIDE), local_mix, precision=highest)
    scale = math.sqrt(NN / SAMPLES) / math.sqrt(BLK * N_WIDE)
    return (mixed.reshape(NN, KCOL) * scale)[sample_rows]
```

```python
import functools
import math

import jax
import jax.numpy as jnp
from jax import lax
from jax.experimental import pallas as pl
from jax.experimental.pallas import tpu as pltpu
from jax.sharding import PartitionSpec as P

REACH = 8
LANES = 128
MESH = pl.DeviceIdType.MESH


def split_bf16(x):
    high = x.astype(jnp.bfloat16)
    return high, (x - high.astype(jnp.float32)).astype(jnp.bfloat16)


def parity_sign(bits, width):
    shift = 1 << max(width - 1, 1).bit_length() >> 1
    while shift:
        bits = bits ^ (bits >> shift)
        shift //= 2
    return (1 - 2 * (bits & 1)).astype(jnp.float32)


def within(value, count):
    return value & (count - 1) if count & (count - 1) == 0 else lax.rem(value, count)


def dot(a, b):
    return jnp.dot(a, b, preferred_element_type=jnp.float32)


def sketch_kernel(
    scale, blocks, vectors, signs, columns, samples, out,
    held_blocks, own, high, low, halo, wide_halo, outside, band, mixed, column_land, column_scalar, row_land,
    row_scalar, partial, first, first_land, second, second_land, third_land,
    local_sem, block_send, block_recv, halo_send, halo_recv, column_send, column_recv, row_send, row_recv,
    y_send, y_recv, z_send, z_recv, x_send, x_recv,
):
    wide = lax.axis_size("wide")
    shares = lax.axis_size("narrow")
    me, part = lax.axis_index("wide"), lax.axis_index("narrow")
    slab_rows, slots, order = blocks.shape[:3]
    slab_total = slab_rows * order
    total_blocks = slab_rows * wide
    width = out.shape[1]
    chunks = width // LANES
    per_slab = out.shape[0]
    reach_rows = REACH * order
    half_rows = slab_rows // 2
    x_me, y_me, z_me = me % 2, me // 2 % 2, me // 4
    z_count = wide // 4

    barrier = pltpu.get_barrier_semaphore()

    def greet(p, carry):
        pl.semaphore_signal(barrier, 1, device_id={"wide": (me + p) % wide}, device_id_type=MESH)
        return carry
    lax.fori_loop(1, wide, greet, 0)
    for p in range(1, shares):
        pl.semaphore_signal(barrier, 1, device_id={"narrow": (part + p) % shares}, device_id_type=MESH)

    own_copy = pltpu.make_async_copy(
        vectors.at[:, pl.ds(pl.multiple_of(part * width, LANES), width)], own, local_sem.at[slab_rows]
    )
    own_copy.start()

    def block_copy(b):
        return pltpu.make_async_copy(blocks.at[b], held_blocks.at[0, b], local_sem.at[b])

    def begin_blocks(b, carry):
        block_copy(b).start()
        return carry
    lax.fori_loop(0, slab_rows, begin_blocks, 0)
    own_columns = pltpu.make_async_copy(columns, column_scalar.at[0], local_sem.at[slab_rows + 1])
    own_columns.start()
    own_samples = pltpu.make_async_copy(samples, row_scalar.at[me], local_sem.at[slab_rows + 2])
    own_samples.start()

    pl.semaphore_wait(barrier, wide - 1 + shares - 1)

    def partner(p):
        return {"narrow": (part + p) % shares}

    def column_copy(p):
        return pltpu.make_async_remote_copy(
            src_ref=columns, dst_ref=column_land.at[p], send_sem=column_send.at[p], recv_sem=column_recv.at[p],
            device_id=partner(p), device_id_type=MESH,
        )

    def row_copy(p):
        return pltpu.make_async_remote_copy(
            src_ref=samples, dst_ref=row_land.at[p], send_sem=row_send.at[p], recv_sem=row_recv.at[p],
            device_id={"wide": (me + p) % wide}, device_id_type=MESH,
        )

    def share_copy(p, b):
        return pltpu.make_async_remote_copy(
            src_ref=blocks.at[b], dst_ref=held_blocks.at[p, b],
            send_sem=block_send.at[p, b], recv_sem=block_recv.at[p, b],
            device_id=partner(p), device_id_type=MESH,
        )

    def halo_copy(q, side):
        start = slab_total - reach_rows if side == 0 else 0
        to = (me + 1) % wide if side == 0 else (me + wide - 1) % wide
        return pltpu.make_async_remote_copy(
            src_ref=vectors.at[pl.ds(start, reach_rows), pl.ds(pl.multiple_of(part * width + q * LANES, LANES), LANES)],
            dst_ref=halo.at[q, side], send_sem=halo_send.at[q, side], recv_sem=halo_recv.at[q, side],
            device_id={"wide": to}, device_id_type=MESH,
        )

    for p in range(1, shares):
        column_copy(p).start()

    def begin_rows(p, carry):
        row_copy(p).start()
        return carry
    lax.fori_loop(1, wide, begin_rows, 0)
    for q in range(chunks):
        for side in range(2):
            halo_copy(q, side).start()

    def begin_shares(b, carry):
        for p in range(1, shares):
            share_copy(p, b).start()
        return carry
    lax.fori_loop(0, slab_rows, begin_shares, 0)

    own_copy.wait()

    def convert(i, carry):
        h, l = split_bf16(own[pl.ds(pl.multiple_of(i * order, order), order), :])
        high[i] = h
        low[i] = l
        return carry
    lax.fori_loop(0, slab_rows, convert, 0)
    high[slab_rows] = jnp.zeros(high.shape[1:], high.dtype)
    low[slab_rows] = jnp.zeros(low.shape[1:], low.dtype)

    own_columns.wait()
    for p in range(1, shares):
        column_copy(p).wait()
        there = pltpu.make_async_copy(column_land.at[p], column_scalar.at[p], local_sem.at[slab_rows + 1])
        there.start()
        there.wait()

    at_row = lax.broadcasted_iota(jnp.int32, (order, order), 0)
    at_column = lax.broadcasted_iota(jnp.int32, (order, order), 1)
    hadamard = parity_sign(at_row & at_column, (order - 1).bit_length())
    entries = [(p, j) for p in range(shares) for j in range(slots)]

    def row(b, carry):
        block_copy(b).wait()
        for p in range(1, shares):
            share_copy(p, b).wait()
        place = []
        for p, j in entries:
            at = column_scalar[p, b, j] - me * slab_rows + REACH
            at = jnp.where(at < 0, at + total_blocks, at)
            place.append(jnp.where(at >= total_blocks, at - total_blocks, at))
        left, left_high, right_high, right_low = [], [], [], []
        for (p, j), at in zip(entries, place):
            a_high, a_low = split_bf16(held_blocks[p, b, j])
            inside = (at >= REACH) & (at < REACH + slab_rows)
            where = jnp.where(inside, at - REACH, slab_rows)
            left.append(jnp.concatenate([a_high, a_low], axis=0))
            left_high.append(a_high)
            right_high.append(high[where])
            right_low.append(low[where])
        both = dot(jnp.concatenate(left, axis=1), jnp.concatenate(right_high, axis=0))
        small = dot(jnp.concatenate(left_high, axis=1), jnp.concatenate(right_low, axis=0))
        product = both[:order] + (both[order:] + small)

        first_out = jnp.where(b < half_rows, 0, REACH + slab_rows)
        for h in range(REACH):
            piece = jnp.zeros((order, order), jnp.float32)
            for (p, j), at in zip(entries, place):
                piece = piece + held_blocks[p, b, j] * (at - first_out == h).astype(jnp.float32)
            outside[:, h * order:(h + 1) * order] = piece

        sign = (2 * signs[b] - 1).astype(jnp.float32)
        mix = (hadamard * sign).astype(jnp.bfloat16)
        mix = jnp.concatenate([mix, mix], axis=1)
        mixed_row = dot(mix, jnp.concatenate(split_bf16(product), axis=0))
        for q in range(chunks):
            mixed[q, pl.ds(pl.multiple_of(b * order, order), order), :] = mixed_row[:, q * LANES:(q + 1) * LANES]
        turned = dot(mix, jnp.concatenate(split_bf16(outside[...]), axis=0))
        t_high, t_low = split_bf16(turned)
        band[b, :order] = t_high
        band[b, order:] = t_low
        return carry
    lax.fori_loop(0, slab_rows, row, 0)

    own_samples.wait()

    def end_rows(p, carry):
        row_copy(p).wait()
        return carry
    lax.fori_loop(1, wide, end_rows, 0)

    def place_copy(p):
        return pltpu.make_async_copy(
            row_land.at[p], row_scalar.at[(me + wide - p) % wide], row_recv.at[p]
        )

    def begin_place(p, carry):
        place_copy(p).start()
        return carry
    lax.fori_loop(1, wide, begin_place, 0)

    def end_place(p, carry):
        place_copy(p).wait()
        return carry
    lax.fori_loop(1, wide, end_place, 0)

    def y_copy(q):
        return pltpu.make_async_remote_copy(
            src_ref=partial.at[q, 1 - y_me], dst_ref=first_land.at[q], send_sem=y_send.at[q], recv_sem=y_recv.at[q],
            device_id={"wide": me + 2 - 4 * y_me}, device_id_type=MESH,
        )

    def z_copy(q, p):
        to = (z_me + p) % z_count
        return pltpu.make_async_remote_copy(
            src_ref=first.at[q, to], dst_ref=second_land.at[q, p],
            send_sem=z_send.at[q, p], recv_sem=z_recv.at[q, p],
            device_id={"wide": to * 4 + me % 4}, device_id_type=MESH,
        )

    def x_copy(q):
        return pltpu.make_async_remote_copy(
            src_ref=second.at[q, 1 - x_me], dst_ref=third_land.at[q], send_sem=x_send.at[q], recv_sem=x_recv.at[q],
            device_id={"wide": me + 1 - 2 * x_me}, device_id_type=MESH,
        )

    group = 8
    for q in range(chunks):
        for side in range(2):
            halo_copy(q, side).wait()

            def widen(i, carry):
                rows = pl.ds(pl.multiple_of(i * order, order), order)
                wide_halo[side, rows, :] = jnp.concatenate(split_bf16(halo[q, side, rows, :]), axis=1)
                return carry
            lax.fori_loop(0, REACH, widen, 0)
        for b in range(slab_rows):
            side = 0 if b < half_rows else 1
            low_h, high_h = (b, REACH) if side == 0 else (0, b + REACH - slab_rows + 1)
            if low_h >= high_h:
                continue
            got = dot(band[b, :, low_h * order:high_h * order], wide_halo[side, low_h * order:high_h * order, :])
            mixed[q, b * order:(b + 1) * order, :] += got[:order, :LANES] + (got[:order, LANES:] + got[order:, :LANES])

        def pick(w, carry):
            sign = parity_sign(w & me, (wide - 1).bit_length())
            for i in range(0, per_slab, group):
                found = [mixed[q, pl.ds(within(row_scalar[w, 0, i + k], slab_total), 1), :] for k in range(group)]
                partial[q, w // 2 % 2, w // 4, w % 2, i:i + group, :] = jnp.concatenate(found, axis=0) * sign
            return carry
        lax.fori_loop(0, wide, pick, 0)
        y_copy(q).start()
        y_copy(q).wait()
        first[q] = partial[q, y_me] + first_land[q]

        def begin_z(p, carry):
            z_copy(q, p).start()
            return carry
        lax.fori_loop(1, z_count, begin_z, 0)
        second[q] = first[q, z_me]

        def end_z(p, carry):
            z_copy(q, p).wait()
            second[q] += second_land[q, p]
            return carry
        lax.fori_loop(1, z_count, end_z, 0)
        x_copy(q).start()
        x_copy(q).wait()
        out[:, q * LANES:(q + 1) * LANES] = (second[q, x_me] + third_land[q]) * scale


def local(blocks, vectors, sign_bits, column_blocks, sample_rows):
    slab_rows, slots, order = blocks.shape[:3]
    wide = lax.axis_size("wide")
    shares = lax.axis_size("narrow")
    width = vectors.shape[1] // shares
    chunks = width // LANES
    slab_total = slab_rows * order
    per_slab = sample_rows.shape[0]
    z_count = wide // 4
    scale = math.sqrt(slab_total / per_slab) / math.sqrt(order * wide)
    hbm = pl.BlockSpec(memory_space=pl.ANY)
    vmem = pl.BlockSpec(memory_space=pltpu.VMEM)
    f32, bf16, i32 = jnp.float32, jnp.bfloat16, jnp.int32
    dma = pltpu.SemaphoreType.DMA
    return pl.pallas_call(
        functools.partial(sketch_kernel, scale),
        in_specs=[hbm, hbm, vmem, vmem, vmem],
        out_specs=vmem,
        out_shape=jax.ShapeDtypeStruct((per_slab, width), f32),
        scratch_shapes=[
            pltpu.VMEM((shares, slab_rows, slots, order, order), f32),
            pltpu.VMEM((slab_total, width), f32),
            pltpu.VMEM((slab_rows + 1, order, width), bf16),
            pltpu.VMEM((slab_rows + 1, order, width), bf16),
            pltpu.VMEM((chunks, 2, REACH * order, LANES), f32),
            pltpu.VMEM((2, REACH * order, 2 * LANES), bf16),
            pltpu.VMEM((order, REACH * order), f32),
            pltpu.VMEM((slab_rows, 2 * order, REACH * order), bf16),
            pltpu.VMEM((chunks, slab_total, LANES), f32),
            pltpu.VMEM((shares, slab_rows, slots), i32),
            pltpu.SMEM((shares, slab_rows, slots), i32),
            pltpu.VMEM((wide, 1, per_slab), i32),
            pltpu.SMEM((wide, 1, per_slab), i32),
            pltpu.VMEM((chunks, 2, z_count, 2, per_slab, LANES), f32),
            pltpu.VMEM((chunks, z_count, 2, per_slab, LANES), f32),
            pltpu.VMEM((chunks, z_count, 2, per_slab, LANES), f32),
            pltpu.VMEM((chunks, 2, per_slab, LANES), f32),
            pltpu.VMEM((chunks, z_count, 2, per_slab, LANES), f32),
            pltpu.VMEM((chunks, per_slab, LANES), f32),
            dma((slab_rows + 3,)),
            dma((shares, slab_rows)),
            dma((shares, slab_rows)),
            dma((chunks, 2)),
            dma((chunks, 2)),
            dma((shares,)),
            dma((shares,)),
            dma((wide,)),
            dma((wide,)),
            dma((chunks,)),
            dma((chunks,)),
            dma((chunks, z_count)),
            dma((chunks, z_count)),
            dma((chunks,)),
            dma((chunks,)),
        ],
        compiler_params=pltpu.CompilerParams(
            has_side_effects=True, collective_id=0, vmem_limit_bytes=60 << 20
        ),
        name="sketch",
    )(blocks, vectors, sign_bits.reshape(slab_rows, 1, order), column_blocks, sample_rows.reshape(1, per_slab))


def solution(mesh):
    return jax.shard_map(
        local,
        mesh=mesh,
        in_specs=(
            P("wide", "narrow", None, None),
            P("wide", None),
            P("wide"),
            P("wide", "narrow"),
            P("wide"),
        ),
        out_specs=P("wide", "narrow"),
        check_vma=False,
    )
```

```python
import functools
import math

import jax
import jax.numpy as jnp
from jax import lax
from jax.experimental import pallas as pl
from jax.experimental.pallas import tpu as pltpu
from jax.sharding import PartitionSpec as P

REACH = 8
LANES = 128
MESH = pl.DeviceIdType.MESH


def split_bf16(x):
    high = x.astype(jnp.bfloat16)
    return high, (x - high.astype(jnp.float32)).astype(jnp.bfloat16)


def parity_sign(bits, width):
    shift = 1 << max(width - 1, 1).bit_length() >> 1
    while shift:
        bits = bits ^ (bits >> shift)
        shift //= 2
    return (1 - 2 * (bits & 1)).astype(jnp.float32)


def within(value, count):
    return value & (count - 1) if count & (count - 1) == 0 else lax.rem(value, count)


def dot(a, b):
    return jnp.dot(a, b, preferred_element_type=jnp.float32)


def sketch_kernel(
    scale, blocks, vectors, signs, columns, samples, out,
    held_blocks, own, high, low, halo, wide_halo, outside, band, mixed, column_land, column_scalar, row_land,
    row_scalar, partial, first, first_land, second, second_land, third_land,
    last_partial, near_land, total, far_land,
    local_sem, block_send, block_recv, halo_send, halo_recv, column_send, column_recv, row_send, row_recv,
    y_send, y_recv, z_send, z_recv, x_send, x_recv,
    near_send, near_recv, far_send, far_recv,
):
    wide = lax.axis_size("wide")
    shares = lax.axis_size("narrow")
    me, part = lax.axis_index("wide"), lax.axis_index("narrow")
    slab_rows, slots, order = blocks.shape[:3]
    slab_total = slab_rows * order
    total_blocks = slab_rows * wide
    width = out.shape[1]
    chunks = width // LANES
    per_slab = out.shape[0]
    reach_rows = REACH * order
    half_rows = slab_rows // 2
    x_me, y_me, z_me, near_me = me % 2, me // 2 % 2, me // 4, me % 4
    z_count = wide // 4

    barrier = pltpu.get_barrier_semaphore()

    def greet(p, carry):
        pl.semaphore_signal(barrier, 1, device_id={"wide": (me + p) % wide}, device_id_type=MESH)
        return carry
    lax.fori_loop(1, wide, greet, 0)
    for p in range(1, shares):
        pl.semaphore_signal(barrier, 1, device_id={"narrow": (part + p) % shares}, device_id_type=MESH)

    own_copy = pltpu.make_async_copy(
        vectors.at[:, pl.ds(pl.multiple_of(part * width, LANES), width)], own, local_sem.at[slab_rows]
    )
    own_copy.start()

    def block_copy(b):
        return pltpu.make_async_copy(blocks.at[b], held_blocks.at[0, b], local_sem.at[b])

    def begin_blocks(b, carry):
        block_copy(b).start()
        return carry
    lax.fori_loop(0, slab_rows, begin_blocks, 0)
    own_columns = pltpu.make_async_copy(columns, column_scalar.at[0], local_sem.at[slab_rows + 1])
    own_columns.start()
    own_samples = pltpu.make_async_copy(samples, row_scalar.at[me], local_sem.at[slab_rows + 2])
    own_samples.start()

    pl.semaphore_wait(barrier, wide - 1 + shares - 1)

    def partner(p):
        return {"narrow": (part + p) % shares}

    def column_copy(p):
        return pltpu.make_async_remote_copy(
            src_ref=columns, dst_ref=column_land.at[p], send_sem=column_send.at[p], recv_sem=column_recv.at[p],
            device_id=partner(p), device_id_type=MESH,
        )

    def row_copy(p):
        return pltpu.make_async_remote_copy(
            src_ref=samples, dst_ref=row_land.at[p], send_sem=row_send.at[p], recv_sem=row_recv.at[p],
            device_id={"wide": (me + p) % wide}, device_id_type=MESH,
        )

    def share_copy(p, b):
        return pltpu.make_async_remote_copy(
            src_ref=blocks.at[b], dst_ref=held_blocks.at[p, b],
            send_sem=block_send.at[p, b], recv_sem=block_recv.at[p, b],
            device_id=partner(p), device_id_type=MESH,
        )

    def halo_copy(q, side):
        start = slab_total - reach_rows if side == 0 else 0
        to = (me + 1) % wide if side == 0 else (me + wide - 1) % wide
        return pltpu.make_async_remote_copy(
            src_ref=vectors.at[pl.ds(start, reach_rows), pl.ds(pl.multiple_of(part * width + q * LANES, LANES), LANES)],
            dst_ref=halo.at[q, side], send_sem=halo_send.at[q, side], recv_sem=halo_recv.at[q, side],
            device_id={"wide": to}, device_id_type=MESH,
        )

    for p in range(1, shares):
        column_copy(p).start()

    def begin_rows(p, carry):
        row_copy(p).start()
        return carry
    lax.fori_loop(1, wide, begin_rows, 0)
    for side in range(2):
        halo_copy(0, side).start()

    def begin_shares(b, carry):
        for p in range(1, shares):
            share_copy(p, b).start()
        return carry
    lax.fori_loop(0, slab_rows, begin_shares, 0)

    own_copy.wait()

    def convert(i, carry):
        h, l = split_bf16(own[pl.ds(pl.multiple_of(i * order, order), order), :])
        high[i] = h
        low[i] = l
        return carry
    lax.fori_loop(0, slab_rows, convert, 0)
    high[slab_rows] = jnp.zeros(high.shape[1:], high.dtype)
    low[slab_rows] = jnp.zeros(low.shape[1:], low.dtype)

    own_columns.wait()
    for p in range(1, shares):
        column_copy(p).wait()
        there = pltpu.make_async_copy(column_land.at[p], column_scalar.at[p], local_sem.at[slab_rows + 1])
        there.start()
        there.wait()

    at_row = lax.broadcasted_iota(jnp.int32, (order, order), 0)
    at_column = lax.broadcasted_iota(jnp.int32, (order, order), 1)
    hadamard = parity_sign(at_row & at_column, (order - 1).bit_length())
    release_row = slab_rows - 3
    entries = [(p, j) for p in range(shares) for j in range(slots)]

    def row(b, carry):
        block_copy(b).wait()
        for p in range(1, shares):
            share_copy(p, b).wait()
        place = []
        for p, j in entries:
            at = column_scalar[p, j, b] - me * slab_rows + REACH
            at = jnp.where(at < 0, at + total_blocks, at)
            place.append(jnp.where(at >= total_blocks, at - total_blocks, at))
        left, left_high, right_high, right_low = [], [], [], []
        for (p, j), at in zip(entries, place):
            a_high, a_low = split_bf16(held_blocks[p, b, j])
            inside = (at >= REACH) & (at < REACH + slab_rows)
            where = jnp.where(inside, at - REACH, slab_rows)
            left.append(jnp.concatenate([a_high, a_low], axis=0))
            left_high.append(a_high)
            right_high.append(high[where])
            right_low.append(low[where])
        both = dot(jnp.concatenate(left, axis=1), jnp.concatenate(right_high, axis=0))
        small = dot(jnp.concatenate(left_high, axis=1), jnp.concatenate(right_low, axis=0))
        product = both[:order] + (both[order:] + small)

        first_out = jnp.where(b < half_rows, 0, REACH + slab_rows)
        for h in range(REACH):
            piece = jnp.zeros((order, order), jnp.float32)
            for (p, j), at in zip(entries, place):
                piece = piece + held_blocks[p, b, j] * (at - first_out == h).astype(jnp.float32)
            outside[:, h * order:(h + 1) * order] = piece

        sign = (2 * signs[b] - 1).astype(jnp.float32)
        mix = (hadamard * sign).astype(jnp.bfloat16)
        mix = jnp.concatenate([mix, mix], axis=1)
        mixed_row = dot(mix, jnp.concatenate(split_bf16(product), axis=0))
        for q in range(chunks):
            mixed[q, pl.ds(pl.multiple_of(b * order, order), order), :] = mixed_row[:, q * LANES:(q + 1) * LANES]
        turned = dot(mix, jnp.concatenate(split_bf16(outside[...]), axis=0))
        t_high, t_low = split_bf16(turned)
        band[b, :order] = t_high
        band[b, order:] = t_low

        @pl.when(b == release_row)
        def _():
            for side in range(2):
                halo_copy(0, side).wait_send()
            for q in range(1, chunks):
                for side in range(2):
                    halo_copy(q, side).start()
        return carry
    lax.fori_loop(0, slab_rows, row, 0)

    own_samples.wait()

    def end_rows(p, carry):
        row_copy(p).wait()
        return carry
    lax.fori_loop(1, wide, end_rows, 0)

    def place_copy(p):
        return pltpu.make_async_copy(
            row_land.at[p], row_scalar.at[(me + wide - p) % wide], row_recv.at[p]
        )

    def begin_place(p, carry):
        place_copy(p).start()
        return carry
    lax.fori_loop(1, wide, begin_place, 0)

    def end_place(p, carry):
        place_copy(p).wait()
        return carry
    lax.fori_loop(1, wide, end_place, 0)

    def y_copy(q):
        return pltpu.make_async_remote_copy(
            src_ref=partial.at[q, 1 - y_me], dst_ref=first_land.at[q], send_sem=y_send.at[q], recv_sem=y_recv.at[q],
            device_id={"wide": me + 2 - 4 * y_me}, device_id_type=MESH,
        )

    def z_copy(q, p):
        to = (z_me + p) % z_count
        return pltpu.make_async_remote_copy(
            src_ref=first.at[q, to], dst_ref=second_land.at[q, p],
            send_sem=z_send.at[q, p], recv_sem=z_recv.at[q, p],
            device_id={"wide": to * 4 + me % 4}, device_id_type=MESH,
        )

    def x_copy(q):
        return pltpu.make_async_remote_copy(
            src_ref=second.at[q, 1 - x_me], dst_ref=third_land.at[q], send_sem=x_send.at[q], recv_sem=x_recv.at[q],
            device_id={"wide": me + 1 - 2 * x_me}, device_id_type=MESH,
        )

    def near_copy(p):
        to = (near_me + p) % 4
        return pltpu.make_async_remote_copy(
            src_ref=last_partial.at[to], dst_ref=near_land.at[p],
            send_sem=near_send.at[p], recv_sem=near_recv.at[p],
            device_id={"wide": z_me * 4 + to}, device_id_type=MESH,
        )

    def far_copy(p):
        to = (z_me + p) % z_count
        return pltpu.make_async_remote_copy(
            src_ref=total.at[to], dst_ref=far_land.at[p],
            send_sem=far_send.at[p], recv_sem=far_recv.at[p],
            device_id={"wide": to * 4 + near_me}, device_id_type=MESH,
        )

    group = 8

    def pick(q, w, to):
        sign = parity_sign(w & me, (wide - 1).bit_length())
        for i in range(0, per_slab, group):
            found = [mixed[q, pl.ds(within(row_scalar[w, 0, i + k], slab_total), 1), :] for k in range(group)]
            to[i:i + group, :] = jnp.concatenate(found, axis=0) * sign

    last = chunks - 1
    for q in range(chunks):
        for side in range(2):
            if q == 0:
                halo_copy(q, side).wait_recv()
            else:
                halo_copy(q, side).wait()

            def widen(i, carry):
                rows = pl.ds(pl.multiple_of(i * order, order), order)
                wide_halo[side, rows, :] = jnp.concatenate(split_bf16(halo[q, side, rows, :]), axis=1)
                return carry
            lax.fori_loop(0, REACH, widen, 0)
        for b in range(slab_rows):
            side = 0 if b < half_rows else 1
            low_h, high_h = (b, REACH) if side == 0 else (0, b + REACH - slab_rows + 1)
            if low_h >= high_h:
                continue
            got = dot(band[b, :, low_h * order:high_h * order], wide_halo[side, low_h * order:high_h * order, :])
            mixed[q, b * order:(b + 1) * order, :] += got[:order, :LANES] + (got[:order, LANES:] + got[order:, :LANES])

        if q < last:
            def pick_one(w, carry):
                pick(q, w, partial.at[q, w // 2 % 2, w // 4, w % 2])
                return carry
            lax.fori_loop(0, wide, pick_one, 0)
            y_copy(q).start()
            y_copy(q).wait()
            first[q] = partial[q, y_me] + first_land[q]

            def begin_z(p, carry):
                z_copy(q, p).start()
                return carry
            lax.fori_loop(1, z_count, begin_z, 0)
        else:
            def pick_near(p, carry):
                to = (near_me + p) % 4

                def pick_far(z, carry):
                    pick(q, z * 4 + to, last_partial.at[to, z])
                    return carry
                lax.fori_loop(0, z_count, pick_far, 0)

                return carry

            def send_near(p, carry):
                pick_near(p, carry)
                near_copy(p).start()
                return carry
            lax.fori_loop(1, 4, send_near, 0)
            pick_near(0, 0)

    for q in range(last):
        second[q] = first[q, z_me]

        def end_z(p, carry):
            z_copy(q, p).wait()
            second[q] += second_land[q, p]
            return carry
        lax.fori_loop(1, z_count, end_z, 0)
        x_copy(q).start()
    total[...] = last_partial[near_me]

    def end_near(p, carry):
        near_copy(p).wait()
        total[...] += near_land[p]
        return carry
    lax.fori_loop(1, 4, end_near, 0)

    def begin_far(p, carry):
        far_copy(p).start()
        return carry
    lax.fori_loop(1, z_count, begin_far, 0)
    for q in range(last):
        x_copy(q).wait()
        out[:, q * LANES:(q + 1) * LANES] = (second[q, x_me] + third_land[q]) * scale
    final = total[z_me]

    def end_far(p, final):
        far_copy(p).wait()
        return final + far_land[p]
    out[:, last * LANES:] = lax.fori_loop(1, z_count, end_far, final) * scale


def local(blocks, vectors, sign_bits, column_blocks, sample_rows):
    slab_rows, slots, order = blocks.shape[:3]
    wide = lax.axis_size("wide")
    shares = lax.axis_size("narrow")
    width = vectors.shape[1] // shares
    chunks = width // LANES
    early = max(chunks - 1, 1)
    slab_total = slab_rows * order
    per_slab = sample_rows.shape[0]
    z_count = wide // 4
    scale = math.sqrt(slab_total / per_slab) / math.sqrt(order * wide)
    hbm = pl.BlockSpec(memory_space=pl.ANY)
    vmem = pl.BlockSpec(memory_space=pltpu.VMEM)
    f32, bf16, i32 = jnp.float32, jnp.bfloat16, jnp.int32
    dma = pltpu.SemaphoreType.DMA
    return pl.pallas_call(
        functools.partial(sketch_kernel, scale),
        in_specs=[hbm, hbm, vmem, vmem, vmem],
        out_specs=vmem,
        out_shape=jax.ShapeDtypeStruct((per_slab, width), f32),
        scratch_shapes=[
            pltpu.VMEM((shares, slab_rows, slots, order, order), f32),
            pltpu.VMEM((slab_total, width), f32),
            pltpu.VMEM((slab_rows + 1, order, width), bf16),
            pltpu.VMEM((slab_rows + 1, order, width), bf16),
            pltpu.VMEM((chunks, 2, REACH * order, LANES), f32),
            pltpu.VMEM((2, REACH * order, 2 * LANES), bf16),
            pltpu.VMEM((order, REACH * order), f32),
            pltpu.VMEM((slab_rows, 2 * order, REACH * order), bf16),
            pltpu.VMEM((chunks, slab_total, LANES), f32),
            pltpu.VMEM((shares, slots, slab_rows), i32),
            pltpu.SMEM((shares, slots, slab_rows), i32),
            pltpu.VMEM((wide, 1, per_slab), i32),
            pltpu.SMEM((wide, 1, per_slab), i32),
            pltpu.VMEM((early, 2, z_count, 2, per_slab, LANES), f32),
            pltpu.VMEM((early, z_count, 2, per_slab, LANES), f32),
            pltpu.VMEM((early, z_count, 2, per_slab, LANES), f32),
            pltpu.VMEM((early, 2, per_slab, LANES), f32),
            pltpu.VMEM((early, z_count, 2, per_slab, LANES), f32),
            pltpu.VMEM((early, per_slab, LANES), f32),
            pltpu.VMEM((4, z_count, per_slab, LANES), f32),
            pltpu.VMEM((4, z_count, per_slab, LANES), f32),
            pltpu.VMEM((z_count, per_slab, LANES), f32),
            pltpu.VMEM((z_count, per_slab, LANES), f32),
            dma((slab_rows + 3,)),
            dma((shares, slab_rows)),
            dma((shares, slab_rows)),
            dma((chunks, 2)),
            dma((chunks, 2)),
            dma((shares,)),
            dma((shares,)),
            dma((wide,)),
            dma((wide,)),
            dma((chunks,)),
            dma((chunks,)),
            dma((chunks, z_count)),
            dma((chunks, z_count)),
            dma((chunks,)),
            dma((chunks,)),
            dma((4,)),
            dma((4,)),
            dma((z_count,)),
            dma((z_count,)),
        ],
        compiler_params=pltpu.CompilerParams(
            has_side_effects=True, collective_id=0, vmem_limit_bytes=60 << 20
        ),
        name="sketch",
    )(blocks, vectors, sign_bits.reshape(slab_rows, 1, order), column_blocks.T, sample_rows.reshape(1, per_slab))


def solution(mesh):
    return jax.shard_map(
        local,
        mesh=mesh,
        in_specs=(
            P("wide", "narrow", None, None),
            P("wide", None),
            P("wide"),
            P("wide", "narrow"),
            P("wide"),
        ),
        out_specs=P("wide", "narrow"),
        check_vma=False,
    )
```

```python
import functools
import math

import jax
import jax.numpy as jnp
from jax import lax
from jax.experimental import pallas as pl
from jax.experimental.pallas import tpu as pltpu
from jax.sharding import PartitionSpec as P

REACH = 8
FAR = 3
NEAR = REACH - FAR
LANES = 128
MESH = pl.DeviceIdType.MESH


def split_bf16(x):
    high = x.astype(jnp.bfloat16)
    return high, (x - high.astype(jnp.float32)).astype(jnp.bfloat16)


def parity(bits, width):
    shift = 1 << max(width - 1, 1).bit_length() >> 1
    while shift:
        bits = bits ^ (bits >> shift)
        shift //= 2
    return bits & 1


def parity_sign(bits, width):
    return (1 - 2 * parity(bits, width)).astype(jnp.float32)


def within(value, count):
    return value & (count - 1) if count & (count - 1) == 0 else lax.rem(value, count)


def dot(a, b):
    return jnp.dot(a, b, preferred_element_type=jnp.float32)


def sketch_kernel(
    scale, blocks, vectors, signs, columns, samples, out,
    held_blocks, own, high, low, halo, wide_halo, outside, outside_far, band, mixed, both_mixed, column_land, column_scalar, row_land,
    row_scalar, partial, first, first_land, second, second_land, third_land,
    last_partial, near_land, total, far_land,
    edge, edge_land, edge_band, edge_product,
    local_sem, block_send, block_recv, halo_send, halo_recv, column_send, column_recv, row_send, row_recv,
    y_send, y_recv, z_send, z_recv, x_send, x_recv,
    near_send, near_recv, far_send, far_recv,
    edge_send, edge_recv, pass_send, pass_recv,
):
    wide = lax.axis_size("wide")
    shares = lax.axis_size("narrow")
    me, part = lax.axis_index("wide"), lax.axis_index("narrow")
    slab_rows, slots, order = blocks.shape[:3]
    slab_total = slab_rows * order
    total_blocks = slab_rows * wide
    width = out.shape[1]
    chunks = width // LANES
    per_slab = out.shape[0]
    near_rows = NEAR * order
    half_rows = slab_rows // 2
    x_me, y_me, z_me, near_me = me % 2, me // 2 % 2, me // 4, me % 4
    z_count = wide // 4

    barrier = pltpu.get_barrier_semaphore()

    def greet(p, carry):
        pl.semaphore_signal(barrier, 1, device_id={"wide": (me + p) % wide}, device_id_type=MESH)
        return carry
    lax.fori_loop(1, wide, greet, 0)
    for p in range(1, shares):
        pl.semaphore_signal(barrier, 1, device_id={"narrow": (part + p) % shares}, device_id_type=MESH)

    own_copy = pltpu.make_async_copy(
        vectors.at[:, pl.ds(pl.multiple_of(part * width, LANES), width)], own, local_sem.at[slab_rows]
    )
    own_copy.start()

    def block_copy(b):
        return pltpu.make_async_copy(blocks.at[b], held_blocks.at[0, b], local_sem.at[b])

    def begin_blocks(b, carry):
        block_copy(b).start()
        return carry
    lax.fori_loop(0, slab_rows, begin_blocks, 0)
    own_columns = pltpu.make_async_copy(columns, column_scalar.at[0], local_sem.at[slab_rows + 1])
    own_columns.start()
    own_samples = pltpu.make_async_copy(samples, row_scalar.at[me], local_sem.at[slab_rows + 2])
    own_samples.start()

    pl.semaphore_wait(barrier, wide - 1 + shares - 1)

    def partner(p):
        return {"narrow": (part + p) % shares}

    def column_copy(p):
        return pltpu.make_async_remote_copy(
            src_ref=columns, dst_ref=column_land.at[p], send_sem=column_send.at[p], recv_sem=column_recv.at[p],
            device_id=partner(p), device_id_type=MESH,
        )

    def row_copy(p):
        return pltpu.make_async_remote_copy(
            src_ref=samples, dst_ref=row_land.at[p], send_sem=row_send.at[p], recv_sem=row_recv.at[p],
            device_id={"wide": (me + p) % wide}, device_id_type=MESH,
        )

    def share_copy(p, b):
        return pltpu.make_async_remote_copy(
            src_ref=blocks.at[b], dst_ref=held_blocks.at[p, b],
            send_sem=block_send.at[p, b], recv_sem=block_recv.at[p, b],
            device_id=partner(p), device_id_type=MESH,
        )

    def halo_copy(q, side):
        start = slab_total - near_rows if side == 0 else 0
        to = (me + 1) % wide if side == 0 else (me + wide - 1) % wide
        return pltpu.make_async_remote_copy(
            src_ref=vectors.at[pl.ds(start, near_rows), pl.ds(pl.multiple_of(part * width + q * LANES, LANES), LANES)],
            dst_ref=halo.at[q, side], send_sem=halo_send.at[q, side], recv_sem=halo_recv.at[q, side],
            device_id={"wide": to}, device_id_type=MESH,
        )

    def edge_span(side, i):
        return pl.ds(i * order, (FAR - i) * order) if side == 0 else pl.ds(0, (i + 1) * order)

    def edge_copy(side, i):
        to = (me + wide - 1) % wide if side == 0 else (me + 1) % wide
        span = edge_span(side, i)
        return pltpu.make_async_remote_copy(
            src_ref=edge.at[side, i, :, span], dst_ref=edge_land.at[side, i, :, span],
            send_sem=edge_send.at[side, i], recv_sem=edge_recv.at[side, i],
            device_id={"wide": to}, device_id_type=MESH,
        )

    def pass_copy(side, i, p):
        span = edge_span(side, i)
        return pltpu.make_async_remote_copy(
            src_ref=edge_land.at[side, i, :, span], dst_ref=edge_land.at[side, i, :, span],
            send_sem=pass_send.at[side, i, p], recv_sem=pass_recv.at[side, i, p],
            device_id=partner(p), device_id_type=MESH,
        )

    for p in range(1, shares):
        column_copy(p).start()

    def begin_rows(p, carry):
        row_copy(p).start()
        return carry
    lax.fori_loop(1, wide, begin_rows, 0)
    for side in range(2):
        halo_copy(0, side).start()

    def row_at(r):
        last_rows = slab_rows - FAR + r - FAR
        return jnp.where(r < FAR, r, jnp.where(r < 2 * FAR, last_rows, r - FAR))

    def begin_shares(r, carry):
        for p in range(1, shares):
            share_copy(p, row_at(r)).start()
        return carry
    lax.fori_loop(0, slab_rows, begin_shares, 0)

    own_copy.wait()

    def convert(i, carry):
        h, l = split_bf16(own[pl.ds(pl.multiple_of(i * order, order), order), :])
        high[i] = h
        low[i] = l
        return carry
    lax.fori_loop(0, slab_rows, convert, 0)
    high[slab_rows] = jnp.zeros(high.shape[1:], high.dtype)
    low[slab_rows] = jnp.zeros(low.shape[1:], low.dtype)

    own_columns.wait()
    for p in range(1, shares):
        column_copy(p).wait()
        there = pltpu.make_async_copy(column_land.at[p], column_scalar.at[p], local_sem.at[slab_rows + 1])
        there.start()
        there.wait()

    at_row = lax.broadcasted_iota(jnp.int32, (order, order), 0)
    at_column = lax.broadcasted_iota(jnp.int32, (order, order), 1)
    hadamard = parity_sign(at_row & at_column, (order - 1).bit_length())
    release_row = slab_rows - 3
    entries = [(p, j) for p in range(shares) for j in range(slots)]

    def row(r, carry):
        b = row_at(r)
        block_copy(b).wait()
        for p in range(1, shares):
            share_copy(p, b).wait()
        place = []
        for p, j in entries:
            at = column_scalar[p, j, b] - me * slab_rows + REACH
            at = jnp.where(at < 0, at + total_blocks, at)
            place.append(jnp.where(at >= total_blocks, at - total_blocks, at))
        left, left_high, right_high, right_low = [], [], [], []
        for (p, j), at in zip(entries, place):
            a_high, a_low = split_bf16(held_blocks[p, b, j])
            inside = (at >= REACH) & (at < REACH + slab_rows)
            where = jnp.where(inside, at - REACH, slab_rows)
            left.append(jnp.concatenate([a_high, a_low], axis=0))
            left_high.append(a_high)
            right_high.append(high[where])
            right_low.append(low[where])
        both = dot(jnp.concatenate(left, axis=1), jnp.concatenate(right_high, axis=0))
        small = dot(jnp.concatenate(left_high, axis=1), jnp.concatenate(right_low, axis=0))
        product = both[:order] + (both[order:] + small)

        def gather(target):
            piece = jnp.zeros((order, order), jnp.float32)
            for (p, j), at in zip(entries, place):
                piece = piece + held_blocks[p, b, j] * (at == target).astype(jnp.float32)
            return piece

        first_near = jnp.where(b < half_rows, FAR, REACH + slab_rows)
        for k in range(NEAR):
            @pl.when(jnp.where(b < half_rows, FAR + k >= b, k <= b + REACH - slab_rows))
            def _():
                outside[:, k * order:(k + 1) * order] = gather(first_near + k)

        sign = (2 * signs[b] - 1).astype(jnp.float32)
        mix = (hadamard * sign).astype(jnp.bfloat16)
        mix = jnp.concatenate([mix, mix], axis=1)
        mixed_row = dot(mix, jnp.concatenate(split_bf16(product), axis=0))
        for q in range(chunks):
            mixed[q, pl.ds(pl.multiple_of(b * order, order), order), :] = mixed_row[:, q * LANES:(q + 1) * LANES]
        turned = dot(mix, jnp.concatenate(split_bf16(outside[...]), axis=0))
        t_high, t_low = split_bf16(turned)
        band[b, :order] = t_high
        band[b, order:] = t_low

        @pl.when(r < 2 * FAR)
        def _():
            side_at = jnp.where(r < FAR, 0, 1)
            first_far = jnp.where(r < FAR, 0, REACH + slab_rows + NEAR)
            for k in range(FAR):
                outside_far[:, k * order:(k + 1) * order] = gather(first_far + k)
            edge[side_at, r - FAR * side_at] = dot(mix, jnp.concatenate(split_bf16(outside_far[...]), axis=0))

        for side in range(2):
            @pl.when((r == (side + 1) * FAR) & (part == side % shares))
            def _():
                for i in range(FAR):
                    edge_copy(side, i).start()

            @pl.when((r == slab_rows - 2) & (part == side % shares))
            def _():
                for i in range(FAR):
                    edge_copy(side, i).wait()
                    for p in range(1, shares):
                        pass_copy(side, i, p).start()

        @pl.when(r == release_row)
        def _():
            for side in range(2):
                halo_copy(0, side).wait_send()
            for q in range(1, chunks):
                for side in range(2):
                    halo_copy(q, side).start()
        return carry
    lax.fori_loop(0, slab_rows, row, 0)

    own_samples.wait()

    def end_rows(p, carry):
        row_copy(p).wait()
        return carry
    lax.fori_loop(1, wide, end_rows, 0)

    def place_copy(p):
        return pltpu.make_async_copy(
            row_land.at[p], row_scalar.at[(me + wide - p) % wide], row_recv.at[p]
        )

    def begin_place(p, carry):
        place_copy(p).start()
        return carry
    lax.fori_loop(1, wide, begin_place, 0)

    def end_place(p, carry):
        place_copy(p).wait()
        return carry
    lax.fori_loop(1, wide, end_place, 0)

    def y_copy(q):
        return pltpu.make_async_remote_copy(
            src_ref=partial.at[q, 1 - y_me], dst_ref=first_land.at[q], send_sem=y_send.at[q], recv_sem=y_recv.at[q],
            device_id={"wide": me + 2 - 4 * y_me}, device_id_type=MESH,
        )

    def z_copy(q, p):
        to = (z_me + p) % z_count
        return pltpu.make_async_remote_copy(
            src_ref=first.at[q, to], dst_ref=second_land.at[q, p],
            send_sem=z_send.at[q, p], recv_sem=z_recv.at[q, p],
            device_id={"wide": to * 4 + me % 4}, device_id_type=MESH,
        )

    def x_copy(q):
        return pltpu.make_async_remote_copy(
            src_ref=second.at[q, 1 - x_me], dst_ref=third_land.at[q], send_sem=x_send.at[q], recv_sem=x_recv.at[q],
            device_id={"wide": me + 1 - 2 * x_me}, device_id_type=MESH,
        )

    def near_copy(p):
        to = (near_me + p) % 4
        return pltpu.make_async_remote_copy(
            src_ref=last_partial.at[to], dst_ref=near_land.at[p],
            send_sem=near_send.at[p], recv_sem=near_recv.at[p],
            device_id={"wide": z_me * 4 + to}, device_id_type=MESH,
        )

    def far_copy(p):
        to = (z_me + p) % z_count
        return pltpu.make_async_remote_copy(
            src_ref=total.at[to], dst_ref=far_land.at[p],
            send_sem=far_send.at[p], recv_sem=far_recv.at[p],
            device_id={"wide": to * 4 + near_me}, device_id_type=MESH,
        )

    for side in range(2):
        for i in range(FAR):
            for p in range(1, shares):
                @pl.when(part == side % shares)
                def _():
                    pass_copy(side, i, p).wait_send()

                @pl.when((part + p) % shares == side % shares)
                def _():
                    pass_copy(side, i, shares - p).wait_recv()
            steps = range(i, FAR) if side == 0 else range(i + 1)
            first_block = slab_rows - REACH if side == 0 else NEAR
            span = slice(steps[0] * order, (steps[-1] + 1) * order)
            edge_high, edge_low = split_bf16(edge_land[side, i, :, span])
            edge_band[side, i, :order, span] = edge_high
            edge_band[side, i, order:, span] = edge_low
            both = dot(
                edge_band[side, i, :, span], jnp.concatenate([high[first_block + k] for k in steps], axis=0)
            )
            small = dot(
                edge_band[side, i, :order, span], jnp.concatenate([low[first_block + k] for k in steps], axis=0)
            )
            edge_product[side, i] = both[:order] + (both[order:] + small)

    group = 8
    index_bits = (wide - 1).bit_length()

    def flipped(w, slab):
        return parity(w & (me ^ slab), index_bits)

    def pick(w, to):
        sign = parity_sign(w & me, index_bits)
        upper = flipped(w, (me + 1) % wide) * slab_total
        lower = flipped(w, (me + wide - 1) % wide) * slab_total

        def found(i):
            at = within(row_scalar[w, 0, i], slab_total)
            return both_mixed[pl.ds(at + jnp.where(at < half_rows * order, upper, lower), 1), :]
        for i in range(0, per_slab, group):
            to[i:i + group, :] = jnp.concatenate([found(i + k) for k in range(group)], axis=0) * sign

    last = chunks - 1
    for q in range(chunks):
        for side in range(2):
            if q == 0:
                halo_copy(q, side).wait_recv()
            else:
                halo_copy(q, side).wait()

            def widen(i, carry):
                rows = pl.ds(pl.multiple_of(i * order, order), order)
                wide_halo[side, rows, :] = jnp.concatenate(split_bf16(halo[q, side, rows, :]), axis=1)
                return carry
            lax.fori_loop(0, NEAR, widen, 0)
        for b in range(slab_rows):
            at = slice(b * order, (b + 1) * order)
            value = mixed[q, at, :]
            if b < half_rows:
                side, begin, end, edge_at = 0, max(b, FAR), REACH, b
            else:
                side, begin, end, edge_at = 1, 0, min(b + REACH - slab_rows + 1, NEAR), b + FAR - slab_rows
            if begin < end:
                shift = FAR if side == 0 else 0
                got = dot(
                    band[b, :, (begin - shift) * order:(end - shift) * order],
                    wide_halo[side, (begin - shift) * order:(end - shift) * order, :],
                )
                value = value + (got[:order, :LANES] + (got[:order, LANES:] + got[order:, :LANES]))
            change = 0
            if 0 <= edge_at < FAR:
                change = edge_product[side, edge_at, :, q * LANES:(q + 1) * LANES]
            both_mixed[at, :] = value + change
            both_mixed[slab_total + b * order:slab_total + (b + 1) * order, :] = value - change

        if q > 0:
            y_copy(q - 1).wait()
            first[q - 1] = partial[q - 1, y_me] + first_land[q - 1]

            def begin_z(p, carry):
                z_copy(q - 1, p).start()
                return carry
            lax.fori_loop(1, z_count, begin_z, 0)
        if q < last:
            def pick_one(w, carry):
                pick(w, partial.at[q, w // 2 % 2, w // 4, w % 2])
                return carry
            lax.fori_loop(0, wide, pick_one, 0)
            y_copy(q).start()
        else:
            def pick_near(p, carry):
                to = (near_me + p) % 4

                def pick_far(z, carry):
                    pick(z * 4 + to, last_partial.at[to, z])
                    return carry
                lax.fori_loop(0, z_count, pick_far, 0)

                return carry

            def send_near(p, carry):
                pick_near(p, carry)
                near_copy(p).start()
                return carry
            lax.fori_loop(1, 4, send_near, 0)
            pick_near(0, 0)

    for q in range(last):
        second[q] = first[q, z_me]

        def end_z(p, carry):
            z_copy(q, p).wait()
            second[q] += second_land[q, p]
            return carry
        lax.fori_loop(1, z_count, end_z, 0)
        x_copy(q).start()
    total[...] = last_partial[near_me]

    def end_near(p, carry):
        near_copy(p).wait()
        total[...] += near_land[p]
        return carry
    lax.fori_loop(1, 4, end_near, 0)

    def begin_far(p, carry):
        far_copy(p).start()
        return carry
    lax.fori_loop(1, z_count, begin_far, 0)
    for q in range(last):
        x_copy(q).wait()
        out[:, q * LANES:(q + 1) * LANES] = (second[q, x_me] + third_land[q]) * scale
    final = total[z_me]

    def end_far(p, final):
        far_copy(p).wait()
        return final + far_land[p]
    out[:, last * LANES:] = lax.fori_loop(1, z_count, end_far, final) * scale


def local(blocks, vectors, sign_bits, column_blocks, sample_rows):
    slab_rows, slots, order = blocks.shape[:3]
    wide = lax.axis_size("wide")
    shares = lax.axis_size("narrow")
    width = vectors.shape[1] // shares
    chunks = width // LANES
    early = max(chunks - 1, 1)
    slab_total = slab_rows * order
    per_slab = sample_rows.shape[0]
    z_count = wide // 4
    scale = math.sqrt(slab_total / per_slab) / math.sqrt(order * wide)
    hbm = pl.BlockSpec(memory_space=pl.ANY)
    vmem = pl.BlockSpec(memory_space=pltpu.VMEM)
    f32, bf16, i32 = jnp.float32, jnp.bfloat16, jnp.int32
    dma = pltpu.SemaphoreType.DMA
    return pl.pallas_call(
        functools.partial(sketch_kernel, scale),
        in_specs=[hbm, hbm, vmem, vmem, vmem],
        out_specs=vmem,
        out_shape=jax.ShapeDtypeStruct((per_slab, width), f32),
        scratch_shapes=[
            pltpu.VMEM((shares, slab_rows, slots, order, order), f32),
            pltpu.VMEM((slab_total, width), f32),
            pltpu.VMEM((slab_rows + 1, order, width), bf16),
            pltpu.VMEM((slab_rows + 1, order, width), bf16),
            pltpu.VMEM((chunks, 2, NEAR * order, LANES), f32),
            pltpu.VMEM((2, NEAR * order, 2 * LANES), bf16),
            pltpu.VMEM((order, NEAR * order), f32),
            pltpu.VMEM((order, FAR * order), f32),
            pltpu.VMEM((slab_rows, 2 * order, NEAR * order), bf16),
            pltpu.VMEM((chunks, slab_total, LANES), f32),
            pltpu.VMEM((2 * slab_total, LANES), f32),
            pltpu.VMEM((shares, slots, slab_rows), i32),
            pltpu.SMEM((shares, slots, slab_rows), i32),
            pltpu.VMEM((wide, 1, per_slab), i32),
            pltpu.SMEM((wide, 1, per_slab), i32),
            pltpu.VMEM((early, 2, z_count, 2, per_slab, LANES), f32),
            pltpu.VMEM((early, z_count, 2, per_slab, LANES), f32),
            pltpu.VMEM((early, z_count, 2, per_slab, LANES), f32),
            pltpu.VMEM((early, 2, per_slab, LANES), f32),
            pltpu.VMEM((early, z_count, 2, per_slab, LANES), f32),
            pltpu.VMEM((early, per_slab, LANES), f32),
            pltpu.VMEM((4, z_count, per_slab, LANES), f32),
            pltpu.VMEM((4, z_count, per_slab, LANES), f32),
            pltpu.VMEM((z_count, per_slab, LANES), f32),
            pltpu.VMEM((z_count, per_slab, LANES), f32),
            pltpu.VMEM((2, FAR, order, FAR * order), f32),
            pltpu.VMEM((2, FAR, order, FAR * order), f32),
            pltpu.VMEM((2, FAR, 2 * order, FAR * order), bf16),
            pltpu.VMEM((2, FAR, order, width), f32),
            dma((slab_rows + 3,)),
            dma((shares, slab_rows)),
            dma((shares, slab_rows)),
            dma((chunks, 2)),
            dma((chunks, 2)),
            dma((shares,)),
            dma((shares,)),
            dma((wide,)),
            dma((wide,)),
            dma((chunks,)),
            dma((chunks,)),
            dma((chunks, z_count)),
            dma((chunks, z_count)),
            dma((chunks,)),
            dma((chunks,)),
            dma((4,)),
            dma((4,)),
            dma((z_count,)),
            dma((z_count,)),
            dma((2, FAR)),
            dma((2, FAR)),
            dma((2, FAR, shares)),
            dma((2, FAR, shares)),
        ],
        compiler_params=pltpu.CompilerParams(
            has_side_effects=True, collective_id=0, vmem_limit_bytes=60 << 20
        ),
        name="sketch",
    )(blocks, vectors, sign_bits.reshape(slab_rows, 1, order), column_blocks.T, sample_rows.reshape(1, per_slab))


def solution(mesh):
    return jax.shard_map(
        local,
        mesh=mesh,
        in_specs=(
            P("wide", "narrow", None, None),
            P("wide", None),
            P("wide"),
            P("wide", "narrow"),
            P("wide"),
        ),
        out_specs=P("wide", "narrow"),
        check_vma=False,
    )
```

```python
import functools
import math

import jax
import jax.numpy as jnp
from jax import lax
from jax.experimental import pallas as pl
from jax.experimental.pallas import tpu as pltpu
from jax.sharding import PartitionSpec as P

REACH = 8
FAR = 2
NEAR = REACH - FAR
LANES = 128
MESH = pl.DeviceIdType.MESH


def split_bf16(x):
    high = x.astype(jnp.bfloat16)
    return high, (x - high.astype(jnp.float32)).astype(jnp.bfloat16)


def parity(bits, width):
    shift = 1 << max(width - 1, 1).bit_length() >> 1
    while shift:
        bits = bits ^ (bits >> shift)
        shift //= 2
    return bits & 1


def parity_sign(bits, width):
    return (1 - 2 * parity(bits, width)).astype(jnp.float32)


def within(value, count):
    return value & (count - 1) if count & (count - 1) == 0 else lax.rem(value, count)


def dot(a, b):
    return jnp.dot(a, b, preferred_element_type=jnp.float32)


def sketch_kernel(
    scale, blocks, vectors, signs, columns, samples, out,
    held_blocks, own, high, low, halo, wide_halo, outside, outside_far, band, mixed, both_mixed, column_land, column_scalar, row_land,
    row_scalar, partial, first, first_land, second, second_land, third_land,
    last_partial, near_land, total, far_land,
    edge, edge_land, edge_band, edge_product,
    local_sem, block_send, block_recv, halo_send, halo_recv, column_send, column_recv, row_send, row_recv,
    y_send, y_recv, z_send, z_recv, x_send, x_recv,
    near_send, near_recv, far_send, far_recv,
    edge_send, edge_recv, pass_send, pass_recv,
):
    wide = lax.axis_size("wide")
    shares = lax.axis_size("narrow")
    me, part = lax.axis_index("wide"), lax.axis_index("narrow")
    slab_rows, slots, order = blocks.shape[:3]
    slab_total = slab_rows * order
    total_blocks = slab_rows * wide
    width = out.shape[1]
    chunks = width // LANES
    per_slab = out.shape[0]
    near_rows = NEAR * order
    half_rows = slab_rows // 2
    x_me, y_me, z_me, near_me = me % 2, me // 2 % 2, me // 4, me % 4
    z_count = wide // 4

    barrier = pltpu.get_barrier_semaphore()

    def greet(p, carry):
        pl.semaphore_signal(barrier, 1, device_id={"wide": (me + p) % wide}, device_id_type=MESH)
        return carry
    lax.fori_loop(1, wide, greet, 0)
    for p in range(1, shares):
        pl.semaphore_signal(barrier, 1, device_id={"narrow": (part + p) % shares}, device_id_type=MESH)

    own_copy = pltpu.make_async_copy(
        vectors.at[:, pl.ds(pl.multiple_of(part * width, LANES), width)], own, local_sem.at[slab_rows]
    )
    own_copy.start()

    def block_copy(b):
        return pltpu.make_async_copy(blocks.at[b], held_blocks.at[0, b], local_sem.at[b])

    def begin_blocks(b, carry):
        block_copy(b).start()
        return carry
    lax.fori_loop(0, slab_rows, begin_blocks, 0)
    own_columns = pltpu.make_async_copy(columns, column_scalar.at[0], local_sem.at[slab_rows + 1])
    own_columns.start()
    own_samples = pltpu.make_async_copy(samples, row_scalar.at[me], local_sem.at[slab_rows + 2])
    own_samples.start()

    pl.semaphore_wait(barrier, wide - 1 + shares - 1)

    def partner(p):
        return {"narrow": (part + p) % shares}

    def column_copy(p):
        return pltpu.make_async_remote_copy(
            src_ref=columns, dst_ref=column_land.at[p], send_sem=column_send.at[p], recv_sem=column_recv.at[p],
            device_id=partner(p), device_id_type=MESH,
        )

    def row_copy(p):
        return pltpu.make_async_remote_copy(
            src_ref=samples, dst_ref=row_land.at[p], send_sem=row_send.at[p], recv_sem=row_recv.at[p],
            device_id={"wide": (me + p) % wide}, device_id_type=MESH,
        )

    def share_copy(p, b):
        return pltpu.make_async_remote_copy(
            src_ref=blocks.at[b], dst_ref=held_blocks.at[p, b],
            send_sem=block_send.at[p, b], recv_sem=block_recv.at[p, b],
            device_id=partner(p), device_id_type=MESH,
        )

    def halo_copy(q, side):
        start = slab_total - near_rows if side == 0 else 0
        to = (me + 1) % wide if side == 0 else (me + wide - 1) % wide
        return pltpu.make_async_remote_copy(
            src_ref=vectors.at[pl.ds(start, near_rows), pl.ds(pl.multiple_of(part * width + q * LANES, LANES), LANES)],
            dst_ref=halo.at[q, side], send_sem=halo_send.at[q, side], recv_sem=halo_recv.at[q, side],
            device_id={"wide": to}, device_id_type=MESH,
        )

    def edge_span(side, i):
        return pl.ds(i * order, (FAR - i) * order) if side == 0 else pl.ds(0, (i + 1) * order)

    def edge_copy(side, i):
        to = (me + wide - 1) % wide if side == 0 else (me + 1) % wide
        span = edge_span(side, i)
        return pltpu.make_async_remote_copy(
            src_ref=edge.at[side, i, :, span], dst_ref=edge_land.at[side, i, :, span],
            send_sem=edge_send.at[side, i], recv_sem=edge_recv.at[side, i],
            device_id={"wide": to}, device_id_type=MESH,
        )

    def pass_copy(side, i, p):
        span = edge_span(side, i)
        return pltpu.make_async_remote_copy(
            src_ref=edge_land.at[side, i, :, span], dst_ref=edge_land.at[side, i, :, span],
            send_sem=pass_send.at[side, i, p], recv_sem=pass_recv.at[side, i, p],
            device_id=partner(p), device_id_type=MESH,
        )

    for p in range(1, shares):
        column_copy(p).start()

    def begin_rows(p, carry):
        row_copy(p).start()
        return carry
    lax.fori_loop(1, wide, begin_rows, 0)
    for side in range(2):
        halo_copy(0, side).start()

    def row_at(r):
        last_rows = slab_rows - FAR + r - FAR
        return jnp.where(r < FAR, r, jnp.where(r < 2 * FAR, last_rows, r - FAR))

    def begin_shares(r, carry):
        for p in range(1, shares):
            share_copy(p, row_at(r)).start()
        return carry
    lax.fori_loop(0, slab_rows, begin_shares, 0)

    own_copy.wait()

    def convert(i, carry):
        h, l = split_bf16(own[pl.ds(pl.multiple_of(i * order, order), order), :])
        high[i] = h
        low[i] = l
        return carry
    lax.fori_loop(0, slab_rows, convert, 0)
    high[slab_rows] = jnp.zeros(high.shape[1:], high.dtype)
    low[slab_rows] = jnp.zeros(low.shape[1:], low.dtype)

    own_columns.wait()
    for p in range(1, shares):
        column_copy(p).wait()
        there = pltpu.make_async_copy(column_land.at[p], column_scalar.at[p], local_sem.at[slab_rows + 1])
        there.start()
        there.wait()

    at_row = lax.broadcasted_iota(jnp.int32, (order, order), 0)
    at_column = lax.broadcasted_iota(jnp.int32, (order, order), 1)
    hadamard = parity_sign(at_row & at_column, (order - 1).bit_length())
    release_row = slab_rows - 3
    entries = [(p, j) for p in range(shares) for j in range(slots)]

    def row(r, carry):
        b = row_at(r)
        block_copy(b).wait()
        for p in range(1, shares):
            share_copy(p, b).wait()
        place = []
        for p, j in entries:
            at = column_scalar[p, j, b] - me * slab_rows + REACH
            at = jnp.where(at < 0, at + total_blocks, at)
            place.append(jnp.where(at >= total_blocks, at - total_blocks, at))
        left, left_high, right_high, right_low = [], [], [], []
        for (p, j), at in zip(entries, place):
            a_high, a_low = split_bf16(held_blocks[p, b, j])
            inside = (at >= REACH) & (at < REACH + slab_rows)
            where = jnp.where(inside, at - REACH, slab_rows)
            left.append(jnp.concatenate([a_high, a_low], axis=0))
            left_high.append(a_high)
            right_high.append(high[where])
            right_low.append(low[where])
        both = dot(jnp.concatenate(left, axis=1), jnp.concatenate(right_high, axis=0))
        small = dot(jnp.concatenate(left_high, axis=1), jnp.concatenate(right_low, axis=0))
        product = both[:order] + (both[order:] + small)

        def gather(target):
            piece = jnp.zeros((order, order), jnp.float32)
            for (p, j), at in zip(entries, place):
                piece = piece + held_blocks[p, b, j] * (at == target).astype(jnp.float32)
            return piece

        first_near = jnp.where(b < half_rows, FAR, REACH + slab_rows)
        for k in range(NEAR):
            @pl.when(jnp.where(b < half_rows, FAR + k >= b, k <= b + REACH - slab_rows))
            def _():
                outside[:, k * order:(k + 1) * order] = gather(first_near + k)

        sign = (2 * signs[b] - 1).astype(jnp.float32)
        mix = (hadamard * sign).astype(jnp.bfloat16)
        mix = jnp.concatenate([mix, mix], axis=1)
        mixed_row = dot(mix, jnp.concatenate(split_bf16(product), axis=0))
        for q in range(chunks):
            mixed[q, pl.ds(pl.multiple_of(b * order, order), order), :] = mixed_row[:, q * LANES:(q + 1) * LANES]
        turned = dot(mix, jnp.concatenate(split_bf16(outside[...]), axis=0))
        t_high, t_low = split_bf16(turned)
        band[b, :order] = t_high
        band[b, order:] = t_low

        @pl.when(r < 2 * FAR)
        def _():
            side_at = jnp.where(r < FAR, 0, 1)
            first_far = jnp.where(r < FAR, 0, REACH + slab_rows + NEAR)
            for k in range(FAR):
                outside_far[:, k * order:(k + 1) * order] = gather(first_far + k)
            edge[side_at, r - FAR * side_at] = dot(mix, jnp.concatenate(split_bf16(outside_far[...]), axis=0))

        for side in range(2):
            @pl.when((r == (side + 1) * FAR) & (part == side % shares))
            def _():
                for i in range(FAR):
                    edge_copy(side, i).start()

            @pl.when((r == slab_rows - 2) & (part == side % shares))
            def _():
                for i in range(FAR):
                    edge_copy(side, i).wait()
                    for p in range(1, shares):
                        pass_copy(side, i, p).start()

        @pl.when(r == release_row)
        def _():
            for side in range(2):
                halo_copy(0, side).wait_send()
            for q in range(1, chunks):
                for side in range(2):
                    halo_copy(q, side).start()
        return carry
    lax.fori_loop(0, slab_rows, row, 0)

    own_samples.wait()

    def end_rows(p, carry):
        row_copy(p).wait()
        return carry
    lax.fori_loop(1, wide, end_rows, 0)

    def place_copy(p):
        return pltpu.make_async_copy(
            row_land.at[p], row_scalar.at[(me + wide - p) % wide], row_recv.at[p]
        )

    def begin_place(p, carry):
        place_copy(p).start()
        return carry
    lax.fori_loop(1, wide, begin_place, 0)

    def end_place(p, carry):
        place_copy(p).wait()
        return carry
    lax.fori_loop(1, wide, end_place, 0)

    def y_copy(q):
        return pltpu.make_async_remote_copy(
            src_ref=partial.at[q, 1 - y_me], dst_ref=first_land.at[q], send_sem=y_send.at[q], recv_sem=y_recv.at[q],
            device_id={"wide": me + 2 - 4 * y_me}, device_id_type=MESH,
        )

    def z_copy(q, p):
        to = (z_me + p) % z_count
        return pltpu.make_async_remote_copy(
            src_ref=first.at[q, to], dst_ref=second_land.at[q, p],
            send_sem=z_send.at[q, p], recv_sem=z_recv.at[q, p],
            device_id={"wide": to * 4 + me % 4}, device_id_type=MESH,
        )

    def x_copy(q):
        return pltpu.make_async_remote_copy(
            src_ref=second.at[q, 1 - x_me], dst_ref=third_land.at[q], send_sem=x_send.at[q], recv_sem=x_recv.at[q],
            device_id={"wide": me + 1 - 2 * x_me}, device_id_type=MESH,
        )

    def near_copy(p):
        to = (near_me + p) % 4
        return pltpu.make_async_remote_copy(
            src_ref=last_partial.at[to], dst_ref=near_land.at[p],
            send_sem=near_send.at[p], recv_sem=near_recv.at[p],
            device_id={"wide": z_me * 4 + to}, device_id_type=MESH,
        )

    def far_copy(p):
        to = (z_me + p) % z_count
        return pltpu.make_async_remote_copy(
            src_ref=total.at[to], dst_ref=far_land.at[p],
            send_sem=far_send.at[p], recv_sem=far_recv.at[p],
            device_id={"wide": to * 4 + near_me}, device_id_type=MESH,
        )

    for side in range(2):
        for i in range(FAR):
            for p in range(1, shares):
                @pl.when(part == side % shares)
                def _():
                    pass_copy(side, i, p).wait_send()

                @pl.when((part + p) % shares == side % shares)
                def _():
                    pass_copy(side, i, shares - p).wait_recv()
            steps = range(i, FAR) if side == 0 else range(i + 1)
            first_block = slab_rows - REACH if side == 0 else NEAR
            span = slice(steps[0] * order, (steps[-1] + 1) * order)
            edge_high, edge_low = split_bf16(edge_land[side, i, :, span])
            edge_band[side, i, :order, span] = edge_high
            edge_band[side, i, order:, span] = edge_low
            both = dot(
                edge_band[side, i, :, span], jnp.concatenate([high[first_block + k] for k in steps], axis=0)
            )
            small = dot(
                edge_band[side, i, :order, span], jnp.concatenate([low[first_block + k] for k in steps], axis=0)
            )
            edge_product[side, i] = both[:order] + (both[order:] + small)

    group = 8
    index_bits = (wide - 1).bit_length()

    def flipped(w, slab):
        return parity(w & (me ^ slab), index_bits)

    def pick(w, to):
        sign = parity_sign(w & me, index_bits)
        upper = flipped(w, (me + 1) % wide) * slab_total
        lower = flipped(w, (me + wide - 1) % wide) * slab_total

        def found(i):
            at = within(row_scalar[w, 0, i], slab_total)
            return both_mixed[pl.ds(at + jnp.where(at < half_rows * order, upper, lower), 1), :]
        for i in range(0, per_slab, group):
            to[i:i + group, :] = jnp.concatenate([found(i + k) for k in range(group)], axis=0) * sign

    last = chunks - 1
    for q in range(chunks):
        for side in range(2):
            if q == 0:
                halo_copy(q, side).wait_recv()
            else:
                halo_copy(q, side).wait()

            def widen(i, carry):
                rows = pl.ds(pl.multiple_of(i * order, order), order)
                wide_halo[side, rows, :] = jnp.concatenate(split_bf16(halo[q, side, rows, :]), axis=1)
                return carry
            lax.fori_loop(0, NEAR, widen, 0)
        for b in range(slab_rows):
            at = slice(b * order, (b + 1) * order)
            value = mixed[q, at, :]
            if b < half_rows:
                side, begin, end, edge_at = 0, max(b, FAR), REACH, b
            else:
                side, begin, end, edge_at = 1, 0, min(b + REACH - slab_rows + 1, NEAR), b + FAR - slab_rows
            if begin < end:
                shift = FAR if side == 0 else 0
                got = dot(
                    band[b, :, (begin - shift) * order:(end - shift) * order],
                    wide_halo[side, (begin - shift) * order:(end - shift) * order, :],
                )
                value = value + (got[:order, :LANES] + (got[:order, LANES:] + got[order:, :LANES]))
            change = 0
            if 0 <= edge_at < FAR:
                change = edge_product[side, edge_at, :, q * LANES:(q + 1) * LANES]
            both_mixed[at, :] = value + change
            both_mixed[slab_total + b * order:slab_total + (b + 1) * order, :] = value - change

        if q > 0:
            y_copy(q - 1).wait()
            first[q - 1] = partial[q - 1, y_me] + first_land[q - 1]

            def begin_z(p, carry):
                z_copy(q - 1, p).start()
                return carry
            lax.fori_loop(1, z_count, begin_z, 0)
        if q < last:
            def pick_one(w, carry):
                pick(w, partial.at[q, w // 2 % 2, w // 4, w % 2])
                return carry
            lax.fori_loop(0, wide, pick_one, 0)
            y_copy(q).start()
        else:
            def pick_near(p, carry):
                to = (near_me + p) % 4

                def pick_far(z, carry):
                    pick(z * 4 + to, last_partial.at[to, z])
                    return carry
                lax.fori_loop(0, z_count, pick_far, 0)

                return carry

            def send_near(p, carry):
                pick_near(p, carry)
                near_copy(p).start()
                return carry
            lax.fori_loop(1, 4, send_near, 0)
            pick_near(0, 0)

    for q in range(last):
        second[q] = first[q, z_me]

        def end_z(p, carry):
            z_copy(q, p).wait()
            second[q] += second_land[q, p]
            return carry
        lax.fori_loop(1, z_count, end_z, 0)
        x_copy(q).start()
    total[...] = last_partial[near_me]

    def end_near(p, carry):
        near_copy(p).wait()
        total[...] += near_land[p]
        return carry
    lax.fori_loop(1, 4, end_near, 0)

    def begin_far(p, carry):
        far_copy(p).start()
        return carry
    lax.fori_loop(1, z_count, begin_far, 0)
    for q in range(last):
        x_copy(q).wait()
        out[:, q * LANES:(q + 1) * LANES] = (second[q, x_me] + third_land[q]) * scale
    final = total[z_me]

    def end_far(p, final):
        far_copy(p).wait()
        return final + far_land[p]
    out[:, last * LANES:] = lax.fori_loop(1, z_count, end_far, final) * scale


def local(blocks, vectors, sign_bits, column_blocks, sample_rows):
    slab_rows, slots, order = blocks.shape[:3]
    wide = lax.axis_size("wide")
    shares = lax.axis_size("narrow")
    width = vectors.shape[1] // shares
    chunks = width // LANES
    early = max(chunks - 1, 1)
    slab_total = slab_rows * order
    per_slab = sample_rows.shape[0]
    z_count = wide // 4
    scale = math.sqrt(slab_total / per_slab) / math.sqrt(order * wide)
    hbm = pl.BlockSpec(memory_space=pl.ANY)
    vmem = pl.BlockSpec(memory_space=pltpu.VMEM)
    f32, bf16, i32 = jnp.float32, jnp.bfloat16, jnp.int32
    dma = pltpu.SemaphoreType.DMA
    return pl.pallas_call(
        functools.partial(sketch_kernel, scale),
        in_specs=[hbm, hbm, vmem, vmem, vmem],
        out_specs=vmem,
        out_shape=jax.ShapeDtypeStruct((per_slab, width), f32),
        scratch_shapes=[
            pltpu.VMEM((shares, slab_rows, slots, order, order), f32),
            pltpu.VMEM((slab_total, width), f32),
            pltpu.VMEM((slab_rows + 1, order, width), bf16),
            pltpu.VMEM((slab_rows + 1, order, width), bf16),
            pltpu.VMEM((chunks, 2, NEAR * order, LANES), f32),
            pltpu.VMEM((2, NEAR * order, 2 * LANES), bf16),
            pltpu.VMEM((order, NEAR * order), f32),
            pltpu.VMEM((order, FAR * order), f32),
            pltpu.VMEM((slab_rows, 2 * order, NEAR * order), bf16),
            pltpu.VMEM((chunks, slab_total, LANES), f32),
            pltpu.VMEM((2 * slab_total, LANES), f32),
            pltpu.VMEM((shares, slots, slab_rows), i32),
            pltpu.SMEM((shares, slots, slab_rows), i32),
            pltpu.VMEM((wide, 1, per_slab), i32),
            pltpu.SMEM((wide, 1, per_slab), i32),
            pltpu.VMEM((early, 2, z_count, 2, per_slab, LANES), f32),
            pltpu.VMEM((early, z_count, 2, per_slab, LANES), f32),
            pltpu.VMEM((early, z_count, 2, per_slab, LANES), f32),
            pltpu.VMEM((early, 2, per_slab, LANES), f32),
            pltpu.VMEM((early, z_count, 2, per_slab, LANES), f32),
            pltpu.VMEM((early, per_slab, LANES), f32),
            pltpu.VMEM((4, z_count, per_slab, LANES), f32),
            pltpu.VMEM((4, z_count, per_slab, LANES), f32),
            pltpu.VMEM((z_count, per_slab, LANES), f32),
            pltpu.VMEM((z_count, per_slab, LANES), f32),
            pltpu.VMEM((2, FAR, order, FAR * order), f32),
            pltpu.VMEM((2, FAR, order, FAR * order), f32),
            pltpu.VMEM((2, FAR, 2 * order, FAR * order), bf16),
            pltpu.VMEM((2, FAR, order, width), f32),
            dma((slab_rows + 3,)),
            dma((shares, slab_rows)),
            dma((shares, slab_rows)),
            dma((chunks, 2)),
            dma((chunks, 2)),
            dma((shares,)),
            dma((shares,)),
            dma((wide,)),
            dma((wide,)),
            dma((chunks,)),
            dma((chunks,)),
            dma((chunks, z_count)),
            dma((chunks, z_count)),
            dma((chunks,)),
            dma((chunks,)),
            dma((4,)),
            dma((4,)),
            dma((z_count,)),
            dma((z_count,)),
            dma((2, FAR)),
            dma((2, FAR)),
            dma((2, FAR, shares)),
            dma((2, FAR, shares)),
        ],
        compiler_params=pltpu.CompilerParams(
            has_side_effects=True, collective_id=0, vmem_limit_bytes=60 << 20
        ),
        name="sketch",
    )(blocks, vectors, sign_bits.reshape(slab_rows, 1, order), column_blocks.T, sample_rows.reshape(1, per_slab))


def solution(mesh):
    return jax.shard_map(
        local,
        mesh=mesh,
        in_specs=(
            P("wide", "narrow", None, None),
            P("wide", None),
            P("wide"),
            P("wide", "narrow"),
            P("wide"),
        ),
        out_specs=P("wide", "narrow"),
        check_vma=False,
    )
```

```python
import functools
import math

import jax
import jax.numpy as jnp
from jax import lax
from jax.experimental import pallas as pl
from jax.experimental.pallas import tpu as pltpu
from jax.sharding import PartitionSpec as P

REACH = 8
FAR = 2
NEAR = REACH - FAR
LANES = 128
MESH = pl.DeviceIdType.MESH


def split_bf16(x):
    high = x.astype(jnp.bfloat16)
    return high, (x - high.astype(jnp.float32)).astype(jnp.bfloat16)


def parity(bits, width):
    shift = 1 << max(width - 1, 1).bit_length() >> 1
    while shift:
        bits = bits ^ (bits >> shift)
        shift //= 2
    return bits & 1


def parity_sign(bits, width):
    return (1 - 2 * parity(bits, width)).astype(jnp.float32)


def within(value, count):
    return value & (count - 1) if count & (count - 1) == 0 else lax.rem(value, count)


def dot(a, b):
    return jnp.dot(a, b, preferred_element_type=jnp.float32)


def sketch_kernel(
    scale, blocks, vectors, signs, columns, samples, out,
    held_blocks, own, high, low, halo, wide_halo, outside, outside_far, band, mixed, both_mixed, column_land, column_scalar, row_land,
    row_scalar, partial, first, first_land, second, second_land, third_land,
    last_partial, near_land, total, far_land,
    edge, edge_land, edge_band, edge_product,
    local_sem, block_send, block_recv, halo_send, halo_recv, column_send, column_recv, row_send, row_recv,
    y_send, y_recv, z_send, z_recv, x_send, x_recv,
    near_send, near_recv, far_send, far_recv,
    edge_send, edge_recv, pass_send, pass_recv,
):
    wide = lax.axis_size("wide")
    shares = lax.axis_size("narrow")
    me, part = lax.axis_index("wide"), lax.axis_index("narrow")
    slab_rows, slots, order = blocks.shape[:3]
    slab_total = slab_rows * order
    total_blocks = slab_rows * wide
    width = out.shape[1]
    chunks = width // LANES
    per_slab = out.shape[0]
    near_rows = NEAR * order
    half_rows = slab_rows // 2
    x_me, y_me, z_me, near_me = me % 2, me // 2 % 2, me // 4, me % 4
    z_count = wide // 4

    barrier = pltpu.get_barrier_semaphore()

    def greet(p, carry):
        pl.semaphore_signal(barrier, 1, device_id={"wide": (me + p) % wide}, device_id_type=MESH)
        return carry
    lax.fori_loop(1, wide, greet, 0)
    for p in range(1, shares):
        pl.semaphore_signal(barrier, 1, device_id={"narrow": (part + p) % shares}, device_id_type=MESH)

    own_copy = pltpu.make_async_copy(
        vectors.at[:, pl.ds(pl.multiple_of(part * width, LANES), width)], own, local_sem.at[slab_rows]
    )
    own_copy.start()

    def block_copy(b):
        return pltpu.make_async_copy(blocks.at[b], held_blocks.at[0, b], local_sem.at[b])

    def begin_blocks(b, carry):
        block_copy(b).start()
        return carry
    lax.fori_loop(0, slab_rows, begin_blocks, 0)
    own_columns = pltpu.make_async_copy(columns, column_scalar.at[0], local_sem.at[slab_rows + 1])
    own_columns.start()
    own_samples = pltpu.make_async_copy(samples, row_scalar.at[me], local_sem.at[slab_rows + 2])
    own_samples.start()

    pl.semaphore_wait(barrier, wide - 1 + shares - 1)

    def partner(p):
        return {"narrow": (part + p) % shares}

    def column_copy(p):
        return pltpu.make_async_remote_copy(
            src_ref=columns, dst_ref=column_land.at[p], send_sem=column_send.at[p], recv_sem=column_recv.at[p],
            device_id=partner(p), device_id_type=MESH,
        )

    def row_copy(p):
        return pltpu.make_async_remote_copy(
            src_ref=samples, dst_ref=row_land.at[p], send_sem=row_send.at[p], recv_sem=row_recv.at[p],
            device_id={"wide": (me + p) % wide}, device_id_type=MESH,
        )

    def share_copy(p, b):
        return pltpu.make_async_remote_copy(
            src_ref=blocks.at[b], dst_ref=held_blocks.at[p, b],
            send_sem=block_send.at[p, b], recv_sem=block_recv.at[p, b],
            device_id=partner(p), device_id_type=MESH,
        )

    def halo_copy(q, side):
        start = slab_total - near_rows if side == 0 else 0
        to = (me + 1) % wide if side == 0 else (me + wide - 1) % wide
        return pltpu.make_async_remote_copy(
            src_ref=vectors.at[pl.ds(start, near_rows), pl.ds(pl.multiple_of(part * width + q * LANES, LANES), LANES)],
            dst_ref=halo.at[q, side], send_sem=halo_send.at[q, side], recv_sem=halo_recv.at[q, side],
            device_id={"wide": to}, device_id_type=MESH,
        )

    def edge_span(side, i):
        return pl.ds(i * order, (FAR - i) * order) if side == 0 else pl.ds(0, (i + 1) * order)

    def edge_copy(side, i):
        to = (me + wide - 1) % wide if side == 0 else (me + 1) % wide
        span = edge_span(side, i)
        return pltpu.make_async_remote_copy(
            src_ref=edge.at[side, i, :, span], dst_ref=edge_land.at[side, i, :, span],
            send_sem=edge_send.at[side, i], recv_sem=edge_recv.at[side, i],
            device_id={"wide": to}, device_id_type=MESH,
        )

    def pass_copy(side, i, p):
        span = edge_span(side, i)
        return pltpu.make_async_remote_copy(
            src_ref=edge_land.at[side, i, :, span], dst_ref=edge_land.at[side, i, :, span],
            send_sem=pass_send.at[side, i, p], recv_sem=pass_recv.at[side, i, p],
            device_id=partner(p), device_id_type=MESH,
        )

    for p in range(1, shares):
        column_copy(p).start()

    def begin_rows(p, carry):
        row_copy(p).start()
        return carry
    lax.fori_loop(1, wide, begin_rows, 0)
    for side in range(2):
        halo_copy(0, side).start()

    def row_at(r):
        last_rows = slab_rows - FAR + r - FAR
        return jnp.where(r < FAR, r, jnp.where(r < 2 * FAR, last_rows, r - FAR))

    def begin_shares(r, carry):
        for p in range(1, shares):
            share_copy(p, row_at(r)).start()
        return carry
    lax.fori_loop(0, slab_rows, begin_shares, 0)

    own_copy.wait()

    def convert(i, carry):
        h, l = split_bf16(own[pl.ds(pl.multiple_of(i * order, order), order), :])
        high[i] = h
        low[i] = l
        return carry
    lax.fori_loop(0, slab_rows, convert, 0)
    high[slab_rows] = jnp.zeros(high.shape[1:], high.dtype)
    low[slab_rows] = jnp.zeros(low.shape[1:], low.dtype)

    own_columns.wait()
    for p in range(1, shares):
        column_copy(p).wait()
        there = pltpu.make_async_copy(column_land.at[p], column_scalar.at[p], local_sem.at[slab_rows + 1])
        there.start()
        there.wait()

    at_row = lax.broadcasted_iota(jnp.int32, (order, order), 0)
    at_column = lax.broadcasted_iota(jnp.int32, (order, order), 1)
    hadamard = parity_sign(at_row & at_column, (order - 1).bit_length())
    release_row = slab_rows - 3
    entries = [(p, j) for p in range(shares) for j in range(slots)]

    def row(r, carry):
        b = row_at(r)
        block_copy(b).wait()
        for p in range(1, shares):
            share_copy(p, b).wait()
        place = []
        for p, j in entries:
            at = column_scalar[p, j, b] - me * slab_rows + REACH
            at = jnp.where(at < 0, at + total_blocks, at)
            place.append(jnp.where(at >= total_blocks, at - total_blocks, at))
        left, left_high, right_high, right_low = [], [], [], []
        for (p, j), at in zip(entries, place):
            a_high, a_low = split_bf16(held_blocks[p, b, j])
            inside = (at >= REACH) & (at < REACH + slab_rows)
            where = jnp.where(inside, at - REACH, slab_rows)
            left.append(jnp.concatenate([a_high, a_low], axis=0))
            left_high.append(a_high)
            right_high.append(high[where])
            right_low.append(low[where])
        both = dot(jnp.concatenate(left, axis=1), jnp.concatenate(right_high, axis=0))
        small = dot(jnp.concatenate(left_high, axis=1), jnp.concatenate(right_low, axis=0))
        product = both[:order] + (both[order:] + small)

        def gather(target):
            piece = jnp.zeros((order, order), jnp.float32)
            for (p, j), at in zip(entries, place):
                piece = piece + held_blocks[p, b, j] * (at == target).astype(jnp.float32)
            return piece

        first_near = jnp.where(b < half_rows, FAR, REACH + slab_rows)
        for k in range(NEAR):
            @pl.when(jnp.where(b < half_rows, FAR + k >= b, k <= b + REACH - slab_rows))
            def _():
                outside[:, k * order:(k + 1) * order] = gather(first_near + k)

        sign = (2 * signs[b] - 1).astype(jnp.float32)
        mix = (hadamard * sign).astype(jnp.bfloat16)
        mix = jnp.concatenate([mix, mix], axis=1)
        mixed_row = dot(mix, jnp.concatenate(split_bf16(product), axis=0))
        for q in range(chunks):
            mixed[q, pl.ds(pl.multiple_of(b * order, order), order), :] = mixed_row[:, q * LANES:(q + 1) * LANES]
        turned = dot(mix, jnp.concatenate(split_bf16(outside[...]), axis=0))
        t_high, t_low = split_bf16(turned)
        band[b, :order] = t_high
        band[b, order:] = t_low

        @pl.when(r < 2 * FAR)
        def _():
            side_at = jnp.where(r < FAR, 0, 1)
            first_far = jnp.where(r < FAR, 0, REACH + slab_rows + NEAR)
            for k in range(FAR):
                outside_far[:, k * order:(k + 1) * order] = gather(first_far + k)
            edge[side_at, r - FAR * side_at] = dot(mix, jnp.concatenate(split_bf16(outside_far[...]), axis=0))

        for side in range(2):
            @pl.when((r == (side + 1) * FAR) & (part == side % shares))
            def _():
                for i in range(FAR):
                    edge_copy(side, i).start()

            @pl.when((r == slab_rows - 2) & (part == side % shares))
            def _():
                for i in range(FAR):
                    edge_copy(side, i).wait()
                    for p in range(1, shares):
                        pass_copy(side, i, p).start()

        @pl.when(r == release_row)
        def _():
            for side in range(2):
                halo_copy(0, side).wait_send()
            for q in range(1, chunks):
                for side in range(2):
                    halo_copy(q, side).start()
        return carry
    lax.fori_loop(0, slab_rows, row, 0)

    own_samples.wait()

    def end_rows(p, carry):
        row_copy(p).wait()
        return carry
    lax.fori_loop(1, wide, end_rows, 0)

    def place_copy(p):
        return pltpu.make_async_copy(
            row_land.at[p], row_scalar.at[(me + wide - p) % wide], row_recv.at[p]
        )

    def begin_place(p, carry):
        place_copy(p).start()
        return carry
    lax.fori_loop(1, wide, begin_place, 0)

    def end_place(p, carry):
        place_copy(p).wait()
        return carry
    lax.fori_loop(1, wide, end_place, 0)

    def y_copy(q):
        return pltpu.make_async_remote_copy(
            src_ref=partial.at[q, 1 - y_me], dst_ref=first_land.at[q], send_sem=y_send.at[q], recv_sem=y_recv.at[q],
            device_id={"wide": me + 2 - 4 * y_me}, device_id_type=MESH,
        )

    def z_copy(q, p):
        to = (z_me + p) % z_count
        return pltpu.make_async_remote_copy(
            src_ref=first.at[q, to], dst_ref=second_land.at[q, p],
            send_sem=z_send.at[q, p], recv_sem=z_recv.at[q, p],
            device_id={"wide": to * 4 + me % 4}, device_id_type=MESH,
        )

    def x_copy(q):
        return pltpu.make_async_remote_copy(
            src_ref=second.at[q, 1 - x_me], dst_ref=third_land.at[q], send_sem=x_send.at[q], recv_sem=x_recv.at[q],
            device_id={"wide": me + 1 - 2 * x_me}, device_id_type=MESH,
        )

    def near_copy(p):
        to = (near_me + p) % 4
        return pltpu.make_async_remote_copy(
            src_ref=last_partial.at[to], dst_ref=near_land.at[p],
            send_sem=near_send.at[p], recv_sem=near_recv.at[p],
            device_id={"wide": z_me * 4 + to}, device_id_type=MESH,
        )

    def far_copy(p):
        to = (z_me + p) % z_count
        return pltpu.make_async_remote_copy(
            src_ref=total.at[to], dst_ref=far_land.at[p],
            send_sem=far_send.at[p], recv_sem=far_recv.at[p],
            device_id={"wide": to * 4 + near_me}, device_id_type=MESH,
        )

    for side in range(2):
        for i in range(FAR):
            for p in range(1, shares):
                @pl.when(part == side % shares)
                def _():
                    pass_copy(side, i, p).wait_send()

                @pl.when((part + p) % shares == side % shares)
                def _():
                    pass_copy(side, i, shares - p).wait_recv()
            steps = range(i, FAR) if side == 0 else range(i + 1)
            first_block = slab_rows - REACH if side == 0 else NEAR
            span = slice(steps[0] * order, (steps[-1] + 1) * order)
            edge_high, edge_low = split_bf16(edge_land[side, i, :, span])
            edge_band[side, i, :order, span] = edge_high
            edge_band[side, i, order:, span] = edge_low
            both = dot(
                edge_band[side, i, :, span], jnp.concatenate([high[first_block + k] for k in steps], axis=0)
            )
            small = dot(
                edge_band[side, i, :order, span], jnp.concatenate([low[first_block + k] for k in steps], axis=0)
            )
            edge_product[side, i] = both[:order] + (both[order:] + small)

    group = 8
    index_bits = (wide - 1).bit_length()

    def flipped(w, slab):
        return parity(w & (me ^ slab), index_bits)

    def pick(w, to):
        sign = parity_sign(w & me, index_bits)
        upper = flipped(w, (me + 1) % wide) * slab_total
        lower = flipped(w, (me + wide - 1) % wide) * slab_total

        def found(i):
            at = within(row_scalar[w, 0, i], slab_total)
            return both_mixed[pl.ds(at + jnp.where(at < half_rows * order, upper, lower), 1), :]
        for i in range(0, per_slab, group):
            to[i:i + group, :] = jnp.concatenate([found(i + k) for k in range(group)], axis=0) * sign

    last = chunks - 1
    for q in range(chunks):
        for side in range(2):
            if q == 0:
                halo_copy(q, side).wait_recv()
            else:
                halo_copy(q, side).wait()

            def widen(i, carry):
                rows = pl.ds(pl.multiple_of(i * order, order), order)
                wide_halo[side, rows, :] = jnp.concatenate(split_bf16(halo[q, side, rows, :]), axis=1)
                return carry
            lax.fori_loop(0, NEAR, widen, 0)
        for b in range(slab_rows):
            at = slice(b * order, (b + 1) * order)
            value = mixed[q, at, :]
            if b < half_rows:
                side, begin, end, edge_at = 0, max(b, FAR), REACH, b
            else:
                side, begin, end, edge_at = 1, 0, min(b + REACH - slab_rows + 1, NEAR), b + FAR - slab_rows
            if begin < end:
                shift = FAR if side == 0 else 0
                got = dot(
                    band[b, :, (begin - shift) * order:(end - shift) * order],
                    wide_halo[side, (begin - shift) * order:(end - shift) * order, :],
                )
                value = value + (got[:order, :LANES] + (got[:order, LANES:] + got[order:, :LANES]))
            change = 0
            if 0 <= edge_at < FAR:
                change = edge_product[side, edge_at, :, q * LANES:(q + 1) * LANES]
            both_mixed[at, :] = value + change
            both_mixed[slab_total + b * order:slab_total + (b + 1) * order, :] = value - change

        if q < last:
            def pick_one(w, carry):
                pick(w, partial.at[q, w // 2 % 2, w // 4, w % 2])
                return carry
            lax.fori_loop(0, wide, pick_one, 0)
            y_copy(q).start()
        else:
            def pick_near(p, carry):
                to = (near_me + p) % 4

                def pick_far(z, carry):
                    pick(z * 4 + to, last_partial.at[to, z])
                    return carry
                lax.fori_loop(0, z_count, pick_far, 0)

                return carry

            def send_near(p, carry):
                pick_near(p, carry)
                near_copy(p).start()
                return carry
            lax.fori_loop(1, 4, send_near, 0)
            for e in range(last):
                y_copy(e).wait()
                first[e] = partial[e, y_me] + first_land[e]

                def begin_z(p, carry):
                    z_copy(e, p).start()
                    return carry
                lax.fori_loop(1, z_count, begin_z, 0)
            pick_near(0, 0)

    for q in range(last):
        second[q] = first[q, z_me]

        def end_z(p, carry):
            z_copy(q, p).wait()
            second[q] += second_land[q, p]
            return carry
        lax.fori_loop(1, z_count, end_z, 0)
        x_copy(q).start()
    total[...] = last_partial[near_me]

    def end_near(p, carry):
        near_copy(p).wait()
        total[...] += near_land[p]
        return carry
    lax.fori_loop(1, 4, end_near, 0)

    def begin_far(p, carry):
        far_copy(p).start()
        return carry
    lax.fori_loop(1, z_count, begin_far, 0)
    for q in range(last):
        x_copy(q).wait()
        out[:, q * LANES:(q + 1) * LANES] = (second[q, x_me] + third_land[q]) * scale
    final = total[z_me]

    def end_far(p, final):
        far_copy(p).wait()
        return final + far_land[p]
    out[:, last * LANES:] = lax.fori_loop(1, z_count, end_far, final) * scale


def local(blocks, vectors, sign_bits, column_blocks, sample_rows):
    slab_rows, slots, order = blocks.shape[:3]
    wide = lax.axis_size("wide")
    shares = lax.axis_size("narrow")
    width = vectors.shape[1] // shares
    chunks = width // LANES
    early = max(chunks - 1, 1)
    slab_total = slab_rows * order
    per_slab = sample_rows.shape[0]
    z_count = wide // 4
    scale = math.sqrt(slab_total / per_slab) / math.sqrt(order * wide)
    hbm = pl.BlockSpec(memory_space=pl.ANY)
    vmem = pl.BlockSpec(memory_space=pltpu.VMEM)
    f32, bf16, i32 = jnp.float32, jnp.bfloat16, jnp.int32
    dma = pltpu.SemaphoreType.DMA
    return pl.pallas_call(
        functools.partial(sketch_kernel, scale),
        in_specs=[hbm, hbm, vmem, vmem, vmem],
        out_specs=vmem,
        out_shape=jax.ShapeDtypeStruct((per_slab, width), f32),
        scratch_shapes=[
            pltpu.VMEM((shares, slab_rows, slots, order, order), f32),
            pltpu.VMEM((slab_total, width), f32),
            pltpu.VMEM((slab_rows + 1, order, width), bf16),
            pltpu.VMEM((slab_rows + 1, order, width), bf16),
            pltpu.VMEM((chunks, 2, NEAR * order, LANES), f32),
            pltpu.VMEM((2, NEAR * order, 2 * LANES), bf16),
            pltpu.VMEM((order, NEAR * order), f32),
            pltpu.VMEM((order, FAR * order), f32),
            pltpu.VMEM((slab_rows, 2 * order, NEAR * order), bf16),
            pltpu.VMEM((chunks, slab_total, LANES), f32),
            pltpu.VMEM((2 * slab_total, LANES), f32),
            pltpu.VMEM((shares, slots, slab_rows), i32),
            pltpu.SMEM((shares, slots, slab_rows), i32),
            pltpu.VMEM((wide, 1, per_slab), i32),
            pltpu.SMEM((wide, 1, per_slab), i32),
            pltpu.VMEM((early, 2, z_count, 2, per_slab, LANES), f32),
            pltpu.VMEM((early, z_count, 2, per_slab, LANES), f32),
            pltpu.VMEM((early, z_count, 2, per_slab, LANES), f32),
            pltpu.VMEM((early, 2, per_slab, LANES), f32),
            pltpu.VMEM((early, z_count, 2, per_slab, LANES), f32),
            pltpu.VMEM((early, per_slab, LANES), f32),
            pltpu.VMEM((4, z_count, per_slab, LANES), f32),
            pltpu.VMEM((4, z_count, per_slab, LANES), f32),
            pltpu.VMEM((z_count, per_slab, LANES), f32),
            pltpu.VMEM((z_count, per_slab, LANES), f32),
            pltpu.VMEM((2, FAR, order, FAR * order), f32),
            pltpu.VMEM((2, FAR, order, FAR * order), f32),
            pltpu.VMEM((2, FAR, 2 * order, FAR * order), bf16),
            pltpu.VMEM((2, FAR, order, width), f32),
            dma((slab_rows + 3,)),
            dma((shares, slab_rows)),
            dma((shares, slab_rows)),
            dma((chunks, 2)),
            dma((chunks, 2)),
            dma((shares,)),
            dma((shares,)),
            dma((wide,)),
            dma((wide,)),
            dma((chunks,)),
            dma((chunks,)),
            dma((chunks, z_count)),
            dma((chunks, z_count)),
            dma((chunks,)),
            dma((chunks,)),
            dma((4,)),
            dma((4,)),
            dma((z_count,)),
            dma((z_count,)),
            dma((2, FAR)),
            dma((2, FAR)),
            dma((2, FAR, shares)),
            dma((2, FAR, shares)),
        ],
        compiler_params=pltpu.CompilerParams(
            has_side_effects=True, collective_id=0, vmem_limit_bytes=60 << 20
        ),
        name="sketch",
    )(blocks, vectors, sign_bits.reshape(slab_rows, 1, order), column_blocks.T, sample_rows.reshape(1, per_slab))


def solution(mesh):
    return jax.shard_map(
        local,
        mesh=mesh,
        in_specs=(
            P("wide", "narrow", None, None),
            P("wide", None),
            P("wide"),
            P("wide", "narrow"),
            P("wide"),
        ),
        out_specs=P("wide", "narrow"),
        check_vma=False,
    )
```
